512 devices in a mesh: freq: 8 (over y, x_lo), cells: 64 (over z, x_hi, core).
Axes of the slice: x: 4 (x_hi: 2, x_lo: 2; x = x_hi * 2 + x_lo), y: 4, z: 16, core: 2. Of those that a mesh axis runs over, the one named last changes fastest.
Arguments:
- jacobian_tiles: bfloat16 [8, 192, 20, 128, 128], P('freq', 'cells'), may hold values from -0.29882812 to 0.29882812
- tip_lists: int32 [192, 20], P('cells'), may hold values from 0 to 31, as said below
- counts: int32 [192], P('cells'), may hold values from 1 to 20, as said below
- residual: bfloat16 [8, 4096], P('freq'), may hold values from -6 to 6
Outputs:
- normal_band: float32 [192, 5, 3, 128, 128], P('cells', None, None, 'freq')
- gradient: float32 [24576], P('cells')
The draws below stay inside these ranges and needn't reach their ends.
Inputs may be any that keep to these rules, and one draw needn't show every extreme that they name: `tip_lists`: each cell block's list names 20 different tip blocks, consecutive modulo 32. The first counts[a] slots of cell block a are live.
All inputs are finite; a program needn't handle non-finite values.
Results may differ from the reference program's by a relative error of at most 0.0003.
Values may be sent and summed in bfloat16 or wider, within the bound.
A program may use at most 64 MiB of HBM per device.

```python
import jax
import jax.numpy as jnp
from jax import lax

TILE = 128
TIPB = 32
FREQS = 8
FOOT = 20
SHIFTS = 4
CB_DEV = 3
NCB = 192
NCELLS = 24576
TIPS = 4096
N_CELLS = 64


def draw_tip_lists(key, part):
    jitter = jax.random.randint(jax.random.fold_in(key, 11), (NCB,), -2, 3, dtype=jnp.int32)
    starts = jnp.arange(NCB, dtype=jnp.int32) * TIPB // NCB + jitter
    lists = (starts[:, None] + jnp.arange(FOOT, dtype=jnp.int32)[None, :]) % TIPB
    return lists.astype(jnp.int32)


def draw_counts(key, part):
    values = jax.random.randint(jax.random.fold_in(key, 21), (NCB,), 1, FOOT + 1, dtype=jnp.int32)
    first_pick = jax.random.randint(jax.random.fold_in(key, 22), (), 0, NCB, dtype=jnp.int32)
    step_pick = jax.random.randint(jax.random.fold_in(key, 23), (), 0, NCB - 1, dtype=jnp.int32)
    second_pick = (first_pick + 1 + step_pick) % NCB
    values = values.at[first_pick].set(FOOT)
    values = values.at[second_pick].set(1)
    return values.astype(jnp.int32)


def steps_of(rng, shape, shards, low, largest):
    def one(dim, parts):
        draws = jax.random.uniform(jax.random.fold_in(jax.random.fold_in(rng, 6), dim), (parts,), jnp.float32, low / len(shards), largest / len(shards))
        return jnp.repeat(jnp.exp(draws), shape[dim] // parts).reshape((-1,) + (1,) * (len(shape) - dim - 1))

    loudness = one(*shards[0])
    for cut in shards[1:]:
        loudness = loudness * one(*cut)
    return loudness


def gaussian(stream_key, shape, scale, limit, split=(), held_as=jnp.bfloat16):
    array = jax.random.normal(stream_key, shape, jnp.float32) * scale
    if len(split) > 0:
        array = steps_of(stream_key, shape, split, -0.22, 0.18) * array
    return jnp.clip(array, min=-limit, max=limit).astype(held_as)


def setup_inputs(seed: int = 0) -> dict:
    seeds = jax.random.split(jax.random.key(seed), 5)
    return {
        "jacobian_tiles": gaussian(seeds[0], (FREQS, NCB, FOOT, TILE, TILE), 0.05, 0.29882812, ((0, 8), (1, 64))),
        "tip_lists": draw_tip_lists(jax.random.fold_in(seeds[4], 71), 0),
        "counts": draw_counts(jax.random.fold_in(seeds[4], 71), 0),
        "residual": gaussian(seeds[3], (FREQS, TIPS), 1.0, 6.0, ((0, 8),)),
    }


def panel_products(local_tiles, local_tips, local_live, far_tiles, far_tips, far_live):
    matches = (local_tips[:, :, None, None] == far_tips[None, None, :, :]).astype(jnp.float32)
    matches = matches * local_live[:, :, None, None] * far_live[None, None, :, :]
    matched = jnp.einsum('apbq,fbqik->fabpik', matches, far_tiles, precision=lax.Precision.HIGHEST)
    return jnp.einsum('fapij,fabpik->abjk', local_tiles, matched, precision=lax.Precision.HIGHEST)


def reference(jacobian_tiles, tip_lists, counts, residual):
    slot_ids = jnp.arange(FOOT, dtype=jnp.int32)
    live_mask = (slot_ids[None, :] < counts[:, None]).astype(jnp.float32)
    tip_ids = jnp.arange(TIPB, dtype=jnp.int32)
    resid_blocks = residual.astype(jnp.float32).reshape(FREQS, TIPB, TILE)

    def one_device(device):
        first = (device * CB_DEV).astype(jnp.int32)
        local_tiles = lax.dynamic_slice_in_dim(jacobian_tiles, first, CB_DEV, 1).astype(jnp.float32)
        local_tips = lax.dynamic_slice_in_dim(tip_lists, first, CB_DEV, 0)
        local_live = lax.dynamic_slice_in_dim(live_mask, first, CB_DEV, 0)
        blocks = []
        for offset in range(SHIFTS + 1):
            far_first = (((device + offset) % N_CELLS) * CB_DEV).astype(jnp.int32)
            far_tiles = lax.dynamic_slice_in_dim(jacobian_tiles, far_first, CB_DEV, 1).astype(jnp.float32)
            far_tips = lax.dynamic_slice_in_dim(tip_lists, far_first, CB_DEV, 0)
            far_live = lax.dynamic_slice_in_dim(live_mask, far_first, CB_DEV, 0)
            blocks.append(panel_products(local_tiles, local_tips, local_live, far_tiles, far_tips, far_live))
        onehot = (local_tips[:, :, None] == tip_ids[None, None, :]).astype(jnp.float32) * local_live[:, :, None]
        picked = jnp.einsum('apt,fti->fapi', onehot, resid_blocks, precision=lax.Precision.HIGHEST)
        grad_part = jnp.einsum('fapij,fapi->aj', local_tiles, picked, precision=lax.Precision.HIGHEST)
        return jnp.stack(blocks, axis=1), grad_part.reshape(CB_DEV * TILE)

    bands, grads = lax.map(one_device, jnp.arange(N_CELLS, dtype=jnp.int32))
    normal_band = bands.reshape(NCB, SHIFTS + 1, CB_DEV, TILE, TILE)
    gradient = grads.reshape(NCELLS)
    return normal_band, gradient
```

```python
import functools

import jax
import jax.numpy as jnp
from jax import lax
from jax.experimental import pallas as pl
from jax.experimental.pallas import tpu as pltpu
from jax.sharding import PartitionSpec as P

SHIFTS = 4
NY = 4
PIECES = 4
MESH = pl.DeviceIdType.MESH


def band_kernel(
    jac, tab_vmem, tab_smem, resid, band, grad,
    own, pan_r1, pan_a, pan_r2, pan_b, far_tab, far_smem,
    dense, own_t, prod, y_in, y_sum, x_in, g_own, g_in, g_sum, g_x,
    s_load, s_tab_s, s_tab_r, s_tab_l, s_zs, s_zr, s_xs, s_xr,
    s_1s, s_1r, s_2s, s_2r, s_ys, s_yr, s_xls, s_xlr, s_gs, s_gr, s_gxs, s_gxr,
):
    blocks, slots = jac.shape[:2]
    tips = resid.shape[1] // 128
    piece = slots // PIECES
    rows = band.shape[3]
    f = lax.axis_index("freq")
    d = lax.axis_index("cells")
    nf = lax.axis_size("freq")
    nd = lax.axis_size("cells")
    y, xl = f // 2, lax.rem(f, 2)
    hi, core = lax.rem(d // 2, 2), lax.rem(d, 2)

    def cell(k):
        return (f, lax.rem(d + k + nd, nd))

    def ydev(dy):
        return (lax.rem(f + 2 * dy, nf), d)

    x_pair = (f, d + 2 - 4 * hi)
    core_pair = (f, d + 1 - 2 * core)
    xl_pair = (f + 1 - 2 * xl, d)

    loads = []
    for b in range(blocks):
        cp = pltpu.make_async_copy(jac.at[b], own[b].at[pl.ds(0, slots)], s_load.at[b])
        cp.start()
        loads.append(cp)

    barrier = pltpu.get_barrier_semaphore()
    partners = [cell(k) for k in range(-SHIFTS, SHIFTS + 1) if k != 0]
    partners += [ydev(dy) for dy in range(1, NY)] + [xl_pair]
    for dev in partners:
        pl.semaphore_signal(barrier, inc=1, device_id=dev, device_id_type=MESH)
    zero = jnp.zeros((128, 128), jnp.bfloat16)
    for panel in (own, pan_r1, pan_a, pan_r2, pan_b):
        for block in panel:
            block[slots] = zero
    pl.semaphore_wait(barrier, len(partners))

    def remote(src, dst, ss, rs, dev):
        return pltpu.make_async_remote_copy(
            src_ref=src, dst_ref=dst, send_sem=ss, recv_sem=rs,
            device_id=dev, device_id_type=MESH)

    tab_copies = [
        remote(tab_vmem, far_tab.at[k - 1], s_tab_s.at[k - 1], s_tab_r.at[k - 1], cell(-k))
        for k in range(1, SHIFTS + 1)]
    for cp in tab_copies:
        cp.start()

    source = [jac.at[b] for b in range(blocks)]

    def z_copy(b, j):
        i, part = b * PIECES + j, pl.ds(j * piece, piece)
        return remote(source[b].at[part], pan_b[b].at[part], s_zs.at[i], s_zr.at[i], cell(-4))

    def x_copy(src, b, j):
        i, part = b * PIECES + j, pl.ds(j * piece, piece)
        return remote(src[b].at[part], pan_a[b].at[part], s_xs.at[i], s_xr.at[i], x_pair)

    def core_copy(src, dst, ss, rs, b):
        part = pl.ds(0, slots)
        return remote(src[b].at[part], dst[b].at[part], ss.at[b], rs.at[b], core_pair)

    for b in range(blocks):
        for j in range(PIECES):
            z_copy(b, j).start()

            @pl.when(hi == 1)
            def _():
                x_copy(source, b, j).start()

    @pl.when(core == 1)
    def _():
        for b in range(blocks):
            core_copy(source, pan_r1, s_1s, s_1r, b).start()

    for cp in loads:
        cp.wait()

    def turn(t, carry):
        at = pl.ds(pl.multiple_of(t * 128, 128), 128)
        for a in range(blocks):
            tile = own[a][tab_smem[a, t]].T
            for g in range(2 * NY):
                own_t[pl.ds((g * blocks + a) * rows, rows), at] = tile[g * rows:(g + 1) * rows]
        return carry

    lax.fori_loop(0, tips, turn, 0)

    def unit_id(k, b):
        return k * blocks + b

    def y_copy(u, dy):
        take = pl.ds(pl.multiple_of(lax.rem(y + dy, NY) * 2 * blocks * rows, 8), 2 * blocks * rows)
        i = u * (NY - 1) + dy - 1
        return remote(prod.at[u, take], y_in.at[u, dy - 1], s_ys.at[i], s_yr.at[i], ydev(dy))

    def xl_copy(u):
        give = pl.ds(pl.multiple_of((1 - xl) * blocks * rows, 8), blocks * rows)
        return remote(y_sum.at[u, give], x_in.at[u], s_xls.at[u], s_xlr.at[u], xl_pair)

    def compute(panel, table, k, b):
        def fill(t, carry):
            dense[pl.ds(pl.multiple_of(t * 128, 128), 128), :] = panel[b][table(b, t)]
            return carry

        lax.fori_loop(0, tips, fill, 0)
        u = unit_id(k, b)
        prod[u] = jnp.dot(own_t[...], dense[...], preferred_element_type=jnp.float32)
        for dy in range(1, NY):
            y_copy(u, dy).start()

    def y_finish(u):
        for dy in range(1, NY):
            y_copy(u, dy).wait_recv()
        mine = pl.ds(pl.multiple_of(y * 2 * blocks * rows, 8), 2 * blocks * rows)
        y_sum[u] = prod[u, mine] + y_in[u, 0] + y_in[u, 1] + y_in[u, 2]
        xl_copy(u).start()

    def x_finish(u):
        xl_copy(u).wait_recv()
        keep = pl.ds(pl.multiple_of(xl * blocks * rows, 8), blocks * rows)
        k, b = u // blocks, u % blocks
        total = y_sum[u, keep] + x_in[u]
        for a in range(blocks):
            band[a, k, b] = total[a * rows:(a + 1) * rows]

    queue = []

    def advance(lag_y, lag_x):
        while len(queue) - advance.y > lag_y:
            y_finish(queue[advance.y])
            advance.y += 1
        while advance.y - advance.x > lag_x:
            x_finish(queue[advance.x])
            advance.x += 1

    advance.y = 0
    advance.x = 0

    r = jnp.broadcast_to(resid[...], (16, resid.shape[1]))
    for b in range(blocks):
        compute(own, lambda b, t: tab_smem[b, t], 0, b)
        queue.append(unit_id(0, b))
        g_own[:, pl.ds(b * 128, 128)] = jnp.dot(
            r, dense[...], preferred_element_type=jnp.float32)[:8]

    def g_copy(dy):
        return remote(g_own, g_in.at[y], s_gs.at[dy - 1], s_gr.at[dy - 1], ydev(dy))

    def g_recv(dy):
        return remote(g_own, g_in.at[lax.rem(y - dy + NY, NY)], s_gs.at[dy - 1], s_gr.at[dy - 1], ydev(dy))

    for dy in range(1, NY):
        g_copy(dy).start()
    g_in[y] = g_own[...]

    for k in range(1, SHIFTS + 1):
        tab_copies[k - 1].wait_recv()
        pltpu.make_async_copy(far_tab.at[k - 1], far_smem.at[k - 1], s_tab_l.at[k - 1]).start()
    for k in range(1, SHIFTS + 1):
        pltpu.make_async_copy(far_tab.at[k - 1], far_smem.at[k - 1], s_tab_l.at[k - 1]).wait()

    for dy in range(1, NY):
        g_recv(dy).wait_recv()
    g_sum[...] = ((g_in[0] + g_in[1]) + g_in[2]) + g_in[3]
    gx_copy = remote(g_sum, g_x, s_gxs.at[0], s_gxr.at[0], xl_pair)
    gx_copy.start()

    far = lambda k: (lambda b, t: far_smem[k - 1, b, t])
    for b in range(blocks):
        for j in range(PIECES):
            z_copy(b, j).wait_recv()

            @pl.when(hi == 0)
            def _():
                x_copy(pan_b, b, j).start()

        @pl.when(core == 0)
        def _():
            core_copy(pan_b, pan_r2, s_2s, s_2r, b).start()

        compute(pan_b, far(4), 4, b)
        queue.append(unit_id(4, b))
        advance(2, 2)
        for j in range(PIECES):
            x_copy(source, b, j).wait_recv()

        @pl.when(core == 0)
        def _():
            core_copy(pan_a, pan_r1, s_1s, s_1r, b).start()

        @pl.when(core == 1)
        def _():
            core_copy(pan_a, pan_r2, s_2s, s_2r, b).start()

        compute(pan_a, far(2), 2, b)
        queue.append(unit_id(2, b))
        advance(2, 2)
        core_copy(source, pan_r1, s_1s, s_1r, b).wait_recv()
        compute(pan_r1, far(1), 1, b)
        queue.append(unit_id(1, b))
        advance(2, 2)
        core_copy(source, pan_r2, s_2s, s_2r, b).wait_recv()
        compute(pan_r2, far(3), 3, b)
        queue.append(unit_id(3, b))
        advance(2, 2)

    gx_copy.wait_recv()
    grad[...] = (g_sum[...] + g_x[...])[:1]
    advance(1, 1)
    advance(0, 0)

    for cp in tab_copies:
        cp.wait_send()
    for b in range(blocks):
        for j in range(PIECES):
            z_copy(b, j).wait_send()
            x_copy(source, b, j).wait_send()
        core_copy(source, pan_r1, s_1s, s_1r, b).wait_send()
        core_copy(source, pan_r2, s_2s, s_2r, b).wait_send()
    for u in range(blocks * (SHIFTS + 1)):
        for dy in range(1, NY):
            y_copy(u, dy).wait_send()
        xl_copy(u).wait_send()
    for dy in range(1, NY):
        g_copy(dy).wait_send()
    gx_copy.wait_send()


def on_device(jacobian_tiles, tip_lists, counts, residual):
    _, blocks, slots, tile, _ = jacobian_tiles.shape
    tips = residual.shape[1] // tile
    nf = lax.axis_size("freq")
    rows = tile // nf
    units = blocks * (SHIFTS + 1)
    width = blocks * tile
    slot_ids = jnp.arange(slots, dtype=jnp.int32)
    live = slot_ids[None, :] < counts[:, None]
    tip_ids = jnp.arange(128, dtype=jnp.int32)
    hit = (tip_lists[:, :, None] == tip_ids[None, None, :]) & live[:, :, None]
    table = jnp.min(jnp.where(hit, slot_ids[None, :, None], slots), axis=1)
    table = jnp.pad(table, ((0, 8 - blocks), (0, 0)))
    dma = pltpu.SemaphoreType.DMA
    bf16, f32 = jnp.bfloat16, jnp.float32
    vm = pltpu.VMEM
    panel = [vm((slots + 1, tile, tile), bf16)] * blocks
    pieces = blocks * PIECES
    band, grad = pl.pallas_call(
        band_kernel,
        out_shape=(
            jax.ShapeDtypeStruct((blocks, SHIFTS + 1, blocks, rows, tile), f32),
            jax.ShapeDtypeStruct((1, width), f32),
        ),
        in_specs=[
            pl.BlockSpec(memory_space=pl.ANY),
            pl.BlockSpec(memory_space=pltpu.VMEM),
            pl.BlockSpec(memory_space=pltpu.SMEM),
            pl.BlockSpec(memory_space=pltpu.VMEM),
        ],
        out_specs=(pl.BlockSpec(memory_space=pltpu.VMEM), pl.BlockSpec(memory_space=pltpu.VMEM)),
        scratch_shapes=[
            panel, panel, panel, panel, panel,
            vm((SHIFTS, 8, 128), jnp.int32), pltpu.SMEM((SHIFTS, 8, 128), jnp.int32),
            vm((tips * tile, tile), bf16), vm((width, tips * tile), bf16),
            vm((units, width, tile), f32), vm((units, NY - 1, width // NY, tile), f32),
            vm((units, width // NY, tile), f32), vm((units, width // nf, tile), f32),
            vm((8, width), f32), vm((NY, 8, width), f32), vm((8, width), f32), vm((8, width), f32),
            dma((blocks,)), dma((SHIFTS,)), dma((SHIFTS,)), dma((SHIFTS,)),
            dma((pieces,)), dma((pieces,)), dma((pieces,)), dma((pieces,)),
            dma((blocks,)), dma((blocks,)), dma((blocks,)), dma((blocks,)),
            dma((units * (NY - 1),)), dma((units * (NY - 1),)), dma((units,)), dma((units,)),
            dma((NY - 1,)), dma((NY - 1,)), dma((1,)), dma((1,)),
        ],
        compiler_params=pltpu.CompilerParams(
            collective_id=0, has_side_effects=True, vmem_limit_bytes=48 * 1024 * 1024),
    )(jacobian_tiles.reshape(blocks, slots, tile, tile), table, table, residual)
    return band, grad.reshape(width)


def solution(mesh):
    placed = (P("freq", "cells", None, None, None), P("cells", None), P("cells"), P("freq", None))
    return jax.shard_map(
        on_device,
        mesh=mesh,
        in_specs=placed,
        out_specs=(P("cells", None, None, "freq", None), P("cells")),
        check_vma=False,
    )
```

```python
import functools

import jax
import jax.numpy as jnp
from jax import lax
from jax.experimental import pallas as pl
from jax.experimental.pallas import tpu as pltpu
from jax.sharding import PartitionSpec as P

SHIFTS = 4
NY = 4
PIECES = 4
MESH = pl.DeviceIdType.MESH


def band_kernel(
    jac, tip_lists, counts, resid_hbm, band, grad,
    own, pan_r1, pan_a, pan_r2, pan_b, resid, tab_vmem, tab_smem, far_tab, far_smem,
    dense, own_t, prod, y_in, y_sum, x_in, g_own, g_in, g_sum, g_x,
    s_load, s_own_tab, s_tab_s, s_tab_r, s_tab_l, s_zs, s_zr, s_xs, s_xr,
    s_1s, s_1r, s_2s, s_2r, s_ys, s_yr, s_xls, s_xlr, s_gs, s_gr, s_gxs, s_gxr,
):
    blocks, slots = jac.shape[:2]
    tips = resid_hbm.shape[1] // 128
    piece = slots // PIECES
    rows = band.shape[3]
    f = lax.axis_index("freq")
    d = lax.axis_index("cells")
    nf = lax.axis_size("freq")
    nd = lax.axis_size("cells")
    y, xl = f // 2, lax.rem(f, 2)
    hi, core = lax.rem(d // 2, 2), lax.rem(d, 2)

    def cell(k):
        return (f, lax.rem(d + k + nd, nd))

    def ydev(dy):
        return (lax.rem(f + 2 * dy, nf), d)

    x_pair = (f, d + 2 - 4 * hi)
    core_pair = (f, d + 1 - 2 * core)
    xl_pair = (f + 1 - 2 * xl, d)

    loads = []
    for b in range(blocks):
        cp = pltpu.make_async_copy(jac.at[b], own[b].at[pl.ds(0, slots)], s_load.at[b])
        cp.start()
        loads.append(cp)

    resid_load = pltpu.make_async_copy(resid_hbm, resid, s_load.at[blocks])
    resid_load.start()

    barrier = pltpu.get_barrier_semaphore()
    partners = [cell(k) for k in range(-SHIFTS, SHIFTS + 1) if k != 0]
    partners += [ydev(dy) for dy in range(1, NY)] + [xl_pair]
    for dev in partners:
        pl.semaphore_signal(barrier, inc=1, device_id=dev, device_id_type=MESH)
    row = lax.broadcasted_iota(jnp.int32, (8, 128), 0)
    tip = lax.broadcasted_iota(jnp.int32, (8, 128), 1)
    table = jnp.full((8, 128), slots, jnp.int32)
    for b in range(blocks):
        for p in range(slots):
            named = jnp.where(p < counts[b], tip_lists[b, p], -1)
            table = jnp.where((row == b) & (tip == named), p, table)
    tab_vmem[...] = table
    own_tab = pltpu.make_async_copy(tab_vmem, tab_smem, s_own_tab.at[0])
    own_tab.start()
    zero = jnp.zeros((128, 128), jnp.bfloat16)
    for panel in (own, pan_r1, pan_a, pan_r2, pan_b):
        for block in panel:
            block[slots] = zero
    pl.semaphore_wait(barrier, len(partners))

    def remote(src, dst, ss, rs, dev):
        return pltpu.make_async_remote_copy(
            src_ref=src, dst_ref=dst, send_sem=ss, recv_sem=rs,
            device_id=dev, device_id_type=MESH)

    tab_copies = [
        remote(tab_vmem, far_tab.at[k - 1], s_tab_s.at[k - 1], s_tab_r.at[k - 1], cell(-k))
        for k in range(1, SHIFTS + 1)]
    for cp in tab_copies:
        cp.start()

    source = [jac.at[b] for b in range(blocks)]

    def z_copy(b, j):
        i, part = b * PIECES + j, pl.ds(j * piece, piece)
        return remote(source[b].at[part], pan_b[b].at[part], s_zs.at[i], s_zr.at[i], cell(-4))

    def x_copy(src, b, j):
        i, part = b * PIECES + j, pl.ds(j * piece, piece)
        return remote(src[b].at[part], pan_a[b].at[part], s_xs.at[i], s_xr.at[i], x_pair)

    def core_copy(src, dst, ss, rs, b):
        part = pl.ds(0, slots)
        return remote(src[b].at[part], dst[b].at[part], ss.at[b], rs.at[b], core_pair)

    for b in range(blocks):
        for j in range(PIECES):
            z_copy(b, j).start()

            @pl.when(hi == 1)
            def _():
                x_copy(source, b, j).start()

    @pl.when(core == 1)
    def _():
        for b in range(blocks):
            core_copy(source, pan_r1, s_1s, s_1r, b).start()

    for cp in loads:
        cp.wait()
    resid_load.wait()
    own_tab.wait()
    own_t[pl.ds(blocks * 128, 16), :] = jnp.broadcast_to(resid[...], (16, tips * 128))

    def turn(t, carry):
        at = pl.ds(pl.multiple_of(t * 128, 128), 128)
        for a in range(blocks):
            tile = own[a][tab_smem[a, t]].T
            for g in range(2 * NY):
                own_t[pl.ds((g * blocks + a) * rows, rows), at] = tile[g * rows:(g + 1) * rows]
        return carry

    lax.fori_loop(0, tips, turn, 0, unroll=2)

    queue = []

    def unit_id(k, b):
        return k * blocks + b

    def y_copy(u, dy):
        take = pl.ds(pl.multiple_of(lax.rem(y + dy, NY) * 2 * blocks * rows, 8), 2 * blocks * rows)
        i = u * (NY - 1) + dy - 1
        return remote(prod.at[u, take], y_in.at[u, dy - 1], s_ys.at[i], s_yr.at[i], ydev(dy))

    def xl_copy(u):
        give = pl.ds(pl.multiple_of((1 - xl) * blocks * rows, 8), blocks * rows)
        return remote(y_sum.at[u, give], x_in.at[u], s_xls.at[u], s_xlr.at[u], xl_pair)

    def fill(panel, table, b, column):
        at = pl.ds(column * 128, 128)

        def step(t, carry):
            dense[pl.ds(pl.multiple_of(t * 128, 128), 128), at] = panel[b][table(b, t)]
            return carry

        lax.fori_loop(0, tips, step, 0, unroll=4)

    def send(u):
        for dy in range(1, NY):
            y_copy(u, dy).start()
        queue.append(u)

    def pair(first, second):
        both = []
        for column, (panel, table, k, b) in enumerate((first, second)):
            fill(panel, table, b, column)
            both.append(unit_id(k, b))
        width = blocks * 128
        out = jnp.dot(own_t[pl.ds(0, width), :], dense[:, pl.ds(0, 256)],
                      preferred_element_type=jnp.float32)
        for column, u in enumerate(both):
            prod[u] = out[:, column * 128:(column + 1) * 128]
            send(u)

    def y_finish(u):
        for dy in range(1, NY):
            y_copy(u, dy).wait_recv()
        mine = pl.ds(pl.multiple_of(y * 2 * blocks * rows, 8), 2 * blocks * rows)
        y_sum[u] = prod[u, mine] + y_in[u, 0] + y_in[u, 1] + y_in[u, 2]
        xl_copy(u).start()

    def x_finish(u):
        xl_copy(u).wait_recv()
        keep = pl.ds(pl.multiple_of(xl * blocks * rows, 8), blocks * rows)
        k, b = u // blocks, u % blocks
        total = y_sum[u, keep] + x_in[u]
        for a in range(blocks):
            band[a, k, b] = total[a * rows:(a + 1) * rows]

    def advance(lag_y, lag_x):
        while len(queue) - advance.y > lag_y:
            y_finish(queue[advance.y])
            advance.y += 1
        while advance.y - advance.x > lag_x:
            x_finish(queue[advance.x])
            advance.x += 1

    advance.y = 0
    advance.x = 0

    for b in range(blocks):
        fill(own, lambda b, t: tab_smem[b, t], b, b)
    out = jnp.dot(own_t[...], dense[...], preferred_element_type=jnp.float32)
    for b in range(blocks):
        prod[unit_id(0, b)] = out[:blocks * 128, b * 128:(b + 1) * 128]
        send(unit_id(0, b))
    g_own[...] = out[blocks * 128:blocks * 128 + 8]

    def g_copy(dy):
        return remote(g_own, g_in.at[y], s_gs.at[dy - 1], s_gr.at[dy - 1], ydev(dy))

    def g_recv(dy):
        return remote(g_own, g_in.at[lax.rem(y - dy + NY, NY)], s_gs.at[dy - 1], s_gr.at[dy - 1], ydev(dy))

    for dy in range(1, NY):
        g_copy(dy).start()
    g_in[y] = g_own[...]

    for k in range(1, SHIFTS + 1):
        tab_copies[k - 1].wait_recv()
        pltpu.make_async_copy(far_tab.at[k - 1], far_smem.at[k - 1], s_tab_l.at[k - 1]).start()
    for k in range(1, SHIFTS + 1):
        pltpu.make_async_copy(far_tab.at[k - 1], far_smem.at[k - 1], s_tab_l.at[k - 1]).wait()

    for dy in range(1, NY):
        g_recv(dy).wait_recv()
    g_sum[...] = ((g_in[0] + g_in[1]) + g_in[2]) + g_in[3]
    gx_copy = remote(g_sum, g_x, s_gxs.at[0], s_gxr.at[0], xl_pair)
    gx_copy.start()

    far = lambda k: (lambda b, t: far_smem[k - 1, b, t])
    for b in range(blocks):
        for j in range(PIECES):
            z_copy(b, j).wait_recv()

            @pl.when(hi == 0)
            def _():
                x_copy(pan_b, b, j).start()

        @pl.when(core == 0)
        def _():
            core_copy(pan_b, pan_r2, s_2s, s_2r, b).start()

        for j in range(PIECES):
            x_copy(source, b, j).wait_recv()

        @pl.when(core == 0)
        def _():
            core_copy(pan_a, pan_r1, s_1s, s_1r, b).start()

        @pl.when(core == 1)
        def _():
            core_copy(pan_a, pan_r2, s_2s, s_2r, b).start()

        pair((pan_b, far(4), 4, b), (pan_a, far(2), 2, b))
        advance(2, 2)
        core_copy(source, pan_r1, s_1s, s_1r, b).wait_recv()
        core_copy(source, pan_r2, s_2s, s_2r, b).wait_recv()
        pair((pan_r1, far(1), 1, b), (pan_r2, far(3), 3, b))
        advance(2, 2)

    gx_copy.wait_recv()
    for b in range(blocks):
        at = pl.ds(b * 128, 128)
        grad[pl.ds(b, 1), :] = g_sum[pl.ds(0, 1), at] + g_x[pl.ds(0, 1), at]
    advance(1, 1)
    advance(0, 0)

    for cp in tab_copies:
        cp.wait_send()
    for b in range(blocks):
        for j in range(PIECES):
            z_copy(b, j).wait_send()
            x_copy(source, b, j).wait_send()
        core_copy(source, pan_r1, s_1s, s_1r, b).wait_send()
        core_copy(source, pan_r2, s_2s, s_2r, b).wait_send()
    for u in range(blocks * (SHIFTS + 1)):
        for dy in range(1, NY):
            y_copy(u, dy).wait_send()
        xl_copy(u).wait_send()
    for dy in range(1, NY):
        g_copy(dy).wait_send()
    gx_copy.wait_send()


def on_device(jacobian_tiles, tip_lists, counts, residual):
    _, blocks, slots, tile, _ = jacobian_tiles.shape
    tips = residual.shape[1] // tile
    nf = lax.axis_size("freq")
    rows = tile // nf
    units = blocks * (SHIFTS + 1)
    width = blocks * tile
    dma = pltpu.SemaphoreType.DMA
    bf16, f32 = jnp.bfloat16, jnp.float32
    vm = pltpu.VMEM
    panel = [vm((slots + 1, tile, tile), bf16)] * blocks
    pieces = blocks * PIECES
    band, grad = pl.pallas_call(
        band_kernel,
        out_shape=(
            jax.ShapeDtypeStruct((blocks, SHIFTS + 1, blocks, rows, tile), f32),
            jax.ShapeDtypeStruct((blocks, tile), f32),
        ),
        in_specs=[
            pl.BlockSpec(memory_space=pltpu.HBM),
            pl.BlockSpec(memory_space=pltpu.SMEM),
            pl.BlockSpec(memory_space=pltpu.SMEM),
            pl.BlockSpec(memory_space=pltpu.HBM),
        ],
        out_specs=(pl.BlockSpec(memory_space=pltpu.VMEM), pl.BlockSpec(memory_space=pltpu.VMEM)),
        scratch_shapes=[
            panel, panel, panel, panel, panel,
            vm((1, tips * tile), bf16), vm((8, 128), jnp.int32), pltpu.SMEM((8, 128), jnp.int32),
            vm((SHIFTS, 8, 128), jnp.int32), pltpu.SMEM((SHIFTS, 8, 128), jnp.int32),
            vm((tips * tile, width), bf16), vm((width + 16, tips * tile), bf16),
            vm((units, width, tile), f32), vm((units, NY - 1, width // NY, tile), f32),
            vm((units, width // NY, tile), f32), vm((units, width // nf, tile), f32),
            vm((8, width), f32), vm((NY, 8, width), f32), vm((8, width), f32), vm((8, width), f32),
            dma((blocks + 1,)), dma((1,)), dma((SHIFTS,)), dma((SHIFTS,)), dma((SHIFTS,)),
            dma((pieces,)), dma((pieces,)), dma((pieces,)), dma((pieces,)),
            dma((blocks,)), dma((blocks,)), dma((blocks,)), dma((blocks,)),
            dma((units * (NY - 1),)), dma((units * (NY - 1),)), dma((units,)), dma((units,)),
            dma((NY - 1,)), dma((NY - 1,)), dma((1,)), dma((1,)),
        ],
        compiler_params=pltpu.CompilerParams(
            collective_id=0, has_side_effects=True, vmem_limit_bytes=63 * 1024 * 1024),
    )(jacobian_tiles.reshape(blocks, slots, tile, tile), tip_lists, counts, residual)
    return band, grad.reshape(width)


def solution(mesh):
    placed = (P("freq", "cells", None, None, None), P("cells", None), P("cells"), P("freq", None))
    return jax.shard_map(
        on_device,
        mesh=mesh,
        in_specs=placed,
        out_specs=(P("cells", None, None, "freq", None), P("cells")),
        check_vma=False,
    )
```

```python
import jax
import jax.numpy as jnp
from jax import lax
from jax.experimental import pallas as pl
from jax.experimental.pallas import tpu as pltpu
from jax.sharding import PartitionSpec as P

SHIFTS = 4
NY = 4
NB = 3
SCALE_ROWS = 16
MESH = pl.DeviceIdType.MESH


def unit_list():
    units = [
        ("own", None, -1, [(a, 0, b) for b in range(NB) for a in range(NB)]),
        ("mate", 0, -1, [(a, 1, b) for b in range(NB) for a in range(NB)]),
    ]
    for s in range(NB):
        grid = [(a, lane, s) for a in range(s + 1) for lane in range(2)]
        grid += [(s, lane, b) for b in range(s) for lane in range(2)]
        units.append(("side", None, s, grid))
        units.append(("cross", None, s, grid))
        for lane in range(2):
            down = [(a, lane, s) for a in range(NB)]
            up = [(s, lane, b) for b in range(NB)]
            units.append(("z", 1 if lane else None, s, down + up))
    return units


UNITS = unit_list()
COUNT = [len(blocks) for _, _, _, blocks in UNITS]
BASE = [sum(COUNT[:u]) for u in range(len(UNITS))]
TOTAL = sum(COUNT)


def band_kernel(
    jac, tip_lists, counts, resid_hbm, band, grad,
    raw, pk0, pk1, mate0, mate1, pan_d, pan_od, pan_u, pan_a, pan_oa,
    resid, tab, tab_smem, far_tab, far_smem, mate_tab, mate_smem,
    dense, left, odd_t, cross_t, prod, coded, y_in, y_sum, x_in, fin_out, fin_in,
    g_own, g_in, g_sum, g_x,
    s_load, s_ts, s_tr, s_tl, s_ds, s_dr, s_us, s_ur, s_as, s_ar, s_ms, s_mr,
    s_ods, s_odr, s_oas, s_oar, s_ys, s_yr, s_xls, s_xlr, s_fs, s_fr, s_gs, s_gr,
):
    slots = jac.shape[1]
    half = slots // 2
    pairs = resid_hbm.shape[1] // 256
    rows = band.shape[3]
    f = lax.axis_index("freq")
    d = lax.axis_index("cells")
    nf = lax.axis_size("freq")
    nd = lax.axis_size("cells")
    y, xl = f // 2, lax.rem(f, 2)
    hi, core = lax.rem(d // 2, 2), lax.rem(d, 2)

    def ydev(dy):
        return (lax.rem(f + 2 * dy, nf), d)

    below = (f, lax.rem(d - 4 + nd, nd))
    above = (f, lax.rem(d + 4, nd))
    x_pair = (f, d + 2 - 4 * hi)
    core_pair = (f, d + 1 - 2 * core)
    xl_pair = (f + 1 - 2 * xl, d)

    loads = []
    for b in range(NB):
        loads.append(pltpu.make_async_copy(jac.at[b], raw[b], s_load.at[b]))
    loads.append(pltpu.make_async_copy(resid_hbm, resid, s_load.at[NB]))
    for cp in loads:
        cp.start()

    barrier = pltpu.get_barrier_semaphore()
    partners = [below, above, x_pair, core_pair] + [ydev(dy) for dy in range(1, NY)] + [xl_pair]
    for dev in partners:
        pl.semaphore_signal(barrier, inc=1, device_id=dev, device_id_type=MESH)

    row = lax.broadcasted_iota(jnp.int32, (8, 128), 0)
    col = lax.broadcasted_iota(jnp.int32, (8, 128), 1)
    place = jnp.full((8, 128), half, jnp.int32)
    slot = jnp.zeros((8, 128), jnp.int32)
    for b in range(NB):
        odd_before = 0
        for p in range(slots):
            name = tip_lists[b, p]
            parity = lax.rem(name, 2)
            rank = jnp.where(parity == 1, odd_before, p - odd_before)
            odd_before = odd_before + parity
            mine = row == parity * 4 + b
            slot = jnp.where(mine & (col == rank), p, slot)
            named = jnp.where(p < counts[b], name // 2, -1)
            place = jnp.where(mine & (col == named), rank, place)
    tab[0] = place
    tab[1] = slot
    own_tab = pltpu.make_async_copy(tab, tab_smem, s_load.at[NB + 1])
    own_tab.start()
    zero = jnp.zeros((128, 128), jnp.bfloat16)
    for panel in (pk0, pk1, mate0, mate1, pan_d, pan_od, pan_u, pan_a, pan_oa):
        for block in panel:
            block[half] = zero
    for cp in loads:
        cp.wait()
    own_tab.wait()

    def pack(b):
        def step(i, carry):
            pk0[b][i] = raw[b][tab_smem[1, b, i]]
            pk1[b][i] = raw[b][tab_smem[1, 4 + b, i]]
            return carry

        lax.fori_loop(0, half, step, 0)

    pack(0)
    pl.semaphore_wait(barrier, len(partners))

    def remote(src, dst, ss, rs, dev):
        return pltpu.make_async_remote_copy(
            src_ref=src, dst_ref=dst, send_sem=ss, recv_sem=rs,
            device_id=dev, device_id_type=MESH)

    live = pl.ds(0, half)

    def panel_copies(src, dst, ss, rs, dev, first=0):
        return [
            remote(src[b].at[live], dst[b].at[live], ss.at[first + b], rs.at[first + b], dev)
            for b in range(NB)]

    d_copy = panel_copies(pk0, pan_d, s_ds, s_dr, below)
    u_copy = panel_copies(pk1, pan_u, s_us, s_ur, above)
    a_copy0 = panel_copies(pk0, pan_a, s_as, s_ar, x_pair)
    a_copy1 = panel_copies(pk1, pan_a, s_as, s_ar, x_pair)
    m_copy = panel_copies(pk0, mate0, s_ms, s_mr, core_pair)
    m_copy += panel_copies(pk1, mate1, s_ms, s_mr, core_pair, NB)
    od_copy = panel_copies(pan_d, pan_od, s_ods, s_odr, core_pair)
    oa_copy = panel_copies(pan_a, pan_oa, s_oas, s_oar, core_pair)
    t_copy = [
        remote(tab.at[0], far_tab.at[i], s_ts.at[i], s_tr.at[i], dev)
        for i, dev in enumerate((core_pair, below, above, x_pair))]
    mt_copy = remote(far_tab.at[pl.ds(1, 3)], mate_tab, s_ts.at[4], s_tr.at[4], core_pair)

    for b in range(NB):
        if b > 0:
            pack(b)
        d_copy[b].start()
        u_copy[b].start()

        @pl.when(hi == 1)
        def _():
            a_copy0[b].start()

        @pl.when(hi == 0)
        def _():
            a_copy1[b].start()

        if b == 0:
            for cp in t_copy:
                cp.start()
        m_copy[b].start()
        m_copy[NB + b].start()

    def turn(panel, table, b, put_tile):
        def step(t, carry):
            at = pl.ds(pl.multiple_of(t * 128, 128), 128)
            put_tile(at, panel[b][table(b, t)].T)
            return carry

        lax.fori_loop(0, pairs, step, 0, unroll=2)

    def fill(panel, table, b, which, lane):
        at = pl.ds(b * 256 + lane * 128, 128)

        def step(t, carry):
            dense[which, pl.ds(pl.multiple_of(t * 128, 128), 128), at] = panel[b][table(b, t)]
            return carry

        lax.fori_loop(0, pairs, step, 0, unroll=4)

    def own_table(parity):
        return lambda b, t: tab_smem[0, parity * 4 + b, t]

    def far_table(i, parity):
        return lambda b, t: far_smem[i, parity * 4 + b, t]

    def mate_table(i, parity):
        return lambda b, t: mate_smem[i - 1, parity * 4 + b, t]

    def put_left(which, b):
        def put(at, tile):
            left[which, pl.ds(b * 128, 128), at] = tile
        return put

    def put_odd(b):
        def put(at, tile):
            odd_t[pl.ds(b * 128, 128), at] = tile
        return put

    def put_cross(b):
        def put(at, tile):
            cross_t[pl.ds(b * 128, 128), at] = tile
        return put

    below_rows = pl.ds(NB * 128, 16)
    for t in range(pairs):
        at = pl.ds(t * 128, 128)
        left[0, below_rows, at] = jnp.broadcast_to(resid[:, pl.ds(t * 256, 128)], (16, 128))
        odd_t[below_rows, at] = jnp.broadcast_to(resid[:, pl.ds(t * 256 + 128, 128)], (16, 128))
    for b in range(NB):
        turn(pk0, own_table(0), b, put_left(0, b))
        turn(pk1, own_table(1), b, put_odd(b))
        fill(pk0, own_table(0), b, 3, 0)
        fill(pk1, own_table(1), b, 1, 0)

    for cp in t_copy:
        cp.wait_recv()
    mt_copy.start()
    far_load = pltpu.make_async_copy(far_tab, far_smem, s_tl.at[0])
    far_load.start()
    far_load.wait()

    def on(u, body):
        which = UNITS[u][1]
        if which is None:
            body()
        else:
            pl.when(core == which)(body)

    def coded_base(u):
        return BASE[u] * 128 + u * NY * SCALE_ROWS

    def y_part(u):
        return COUNT[u] * 2 * rows + SCALE_ROWS

    def y_copy(u, dy):
        part = y_part(u)
        take = pl.ds(pl.multiple_of(coded_base(u) + lax.rem(y + dy, NY) * part, 16), part)
        i = u * (NY - 1) + dy - 1
        return remote(coded.at[take], y_in.at[dy - 1, pl.ds(coded_base(u) // NY, part)],
                      s_ys.at[i], s_yr.at[i], ydev(dy))

    def xl_copy(u):
        part = rows * COUNT[u]
        give = pl.ds(pl.multiple_of(BASE[u] * 2 * rows + (1 - xl) * part, 8), part)
        return remote(y_sum.at[give], x_in.at[pl.ds(BASE[u] * rows, part)],
                      s_xls.at[u], s_xlr.at[u], xl_pair)

    def fin_copy(u):
        kind = UNITS[u][0]
        if kind == "z":
            part = pl.ds((BASE[u] + NB) * rows, rows * NB)
        else:
            part = pl.ds(BASE[u] * rows, rows * COUNT[u])
        dev = x_pair if kind == "cross" else below
        return remote(fin_out.at[part], fin_in.at[part], s_fs.at[u], s_fr.at[u], dev)

    def send(u):
        n = COUNT[u]

        def body():
            def peak(i, top):
                at = pl.ds(pl.multiple_of(BASE[u] * 128 + i * 128, 128), 128)
                return jnp.maximum(top, jnp.abs(prod[at]))

            top = lax.fori_loop(0, n, peak, jnp.zeros((128, 128), jnp.float32))
            top = jnp.full((16, 128), jnp.max(top), jnp.float32)
            power = jnp.ceil(jnp.log2(jnp.maximum(top, 1e-33)) + 1e-3)
            up = jnp.exp2(15.0 - power)[:1] * (32766.0 / 32768.0)
            for part in range(NY):
                start = coded_base(u) + part * y_part(u)

                def code(i, carry):
                    src = pl.ds(pl.multiple_of(BASE[u] * 128 + part * n * 32 + i * 32, 32), 32)
                    dst = pl.ds(pl.multiple_of(start + i * 32, 16), 32)
                    coded[dst] = jnp.round(prod[src] * up).astype(jnp.int32).astype(jnp.int16)
                    return carry

                lax.fori_loop(0, n, code, 0)
                coded[pl.ds(start + n * 32, SCALE_ROWS)] = power.astype(jnp.int32).astype(jnp.int16)
            for dy in range(1, NY):
                y_copy(u, dy).start()

        on(u, body)

    def y_finish(u):
        n = COUNT[u]

        def body():
            down = []
            for dy in range(1, NY):
                y_copy(u, dy).wait_recv()
                power = y_in[dy - 1, pl.ds(coded_base(u) // NY + n * 32, SCALE_ROWS)]
                power = power.astype(jnp.int32).astype(jnp.float32)
                down.append(jnp.exp2(power - 15.0)[:1] * (32768.0 / 32766.0))

            def step(i, carry):
                at = pl.ds(pl.multiple_of(BASE[u] * 128 + y * n * 32 + i * 32, 32), 32)
                total = prod[at]
                for dy in range(1, NY):
                    src = pl.ds(pl.multiple_of(coded_base(u) // NY + i * 32, 16), 32)
                    part = y_in[dy - 1, src].astype(jnp.int32).astype(jnp.float32)
                    total = total + part * down[dy - 1]
                y_sum[pl.ds(pl.multiple_of(BASE[u] * 32 + i * 32, 32), 32)] = total
                return carry

            lax.fori_loop(0, n, step, 0)
            xl_copy(u).start()

        on(u, body)

    def block_rows(u, i):
        return pl.ds((BASE[u] + i) * rows, rows)

    def x_finish(u):
        kind, _, _, blocks = UNITS[u]
        part = rows * COUNT[u]

        def body():
            xl_copy(u).wait_recv()
            keep = pl.ds(pl.multiple_of(BASE[u] * 2 * rows + xl * part, 8), part)
            fin_out[pl.ds(BASE[u] * rows, part)] = y_sum[keep] + x_in[pl.ds(BASE[u] * rows, part)]
            if kind == "side":
                pl.when(hi == 1)(lambda: fin_copy(u).start())
            elif kind in ("cross", "z"):
                fin_copy(u).start()

        on(u, body)

    def fin_finish(u):
        kind, _, _, blocks = UNITS[u]

        def body():
            if kind in ("own", "mate"):
                for i, (a, lane, b) in enumerate(blocks):
                    band[a, lane, b] = fin_out[block_rows(u, i)]
            elif kind == "z":
                for i, (a, lane, b) in enumerate(blocks[:NB]):
                    z_own[(a, lane, b)] = (u, i)
                fin_copy(u).wait_recv()
            elif kind == "side":
                def from_here():
                    for i, (a, lane, b) in enumerate(blocks):
                        band[a, 3 - 2 * core if lane else 2, b] = fin_out[block_rows(u, i)]

                def from_above():
                    fin_copy(u).wait_recv()
                    for i, (a, lane, b) in enumerate(blocks):
                        band[a, 3 - 2 * core if lane else 2, b] = fin_in[block_rows(u, i)]

                pl.when(hi == 0)(from_here)
                pl.when(hi == 1)(from_above)
            else:
                fin_copy(u).wait_recv()
                for i, (a, lane, b) in enumerate(blocks):
                    k = 3 - 2 * core if lane else 2
                    band[a, k, b] = band[a, k, b] + fin_in[block_rows(u, i)]

        on(u, body)

    z_own = {}

    def z_place(u):
        _, _, _, blocks = UNITS[u]

        def body():
            for i, (a, lane, b) in enumerate(blocks[NB:]):
                v, j = z_own[(a, lane, b)]
                k = 3 if lane else 4
                band[a, k, b] = fin_out[block_rows(v, j)] + fin_in[block_rows(u, NB + i)]

        on(u, body)

    def put(u, i, block):
        for g in range(2 * NY):
            at = pl.ds(BASE[u] * 128 + (g * COUNT[u] + i) * rows, rows)
            prod[at] = block[g * rows:(g + 1) * rows]

    def put_grid(u, out, rows_of, cols_of):
        for i, (a, lane, b) in enumerate(UNITS[u][3]):
            if a in rows_of and b in cols_of:
                r, c = rows_of.index(a) * 128, cols_of.index(b) * 256 + lane * 128
                put(u, i, out[r:r + 128, c:c + 128])

    def dot(a, b):
        return jnp.dot(a, b, preferred_element_type=jnp.float32)

    for b in range(NB):
        m_copy[b].wait_recv()
        m_copy[NB + b].wait_recv()
        fill(mate0, far_table(0, 0), b, 3, 1)
        fill(mate1, far_table(0, 1), b, 1, 1)
        at = pl.ds(b * 256, 256)
        out = dot(left[0], dense[3, :, at]) + dot(odd_t[...], dense[1, :, at])
        for a in range(NB):
            put(0, b * NB + a, out[a * 128:(a + 1) * 128, :128])
            put(1, b * NB + a, out[a * 128:(a + 1) * 128, 128:])
        g_own[:, pl.ds(b * 128, 128)] = out[NB * 128:NB * 128 + 8, :128]
    send(0)
    send(1)

    def g_copy(dy):
        return remote(g_own, g_in.at[y], s_gs.at[dy - 1], s_gr.at[dy - 1], ydev(dy))

    def g_recv(dy):
        return remote(g_own, g_in.at[lax.rem(y - dy + NY, NY)], s_gs.at[dy - 1], s_gr.at[dy - 1], ydev(dy))

    gx_copy = remote(g_sum, g_x, s_gs.at[NY - 1], s_gr.at[NY - 1], xl_pair)
    for dy in range(1, NY):
        g_copy(dy).start()
    g_in[y] = g_own[...]

    mt_copy.wait_recv()
    mate_load = pltpu.make_async_copy(mate_tab, mate_smem, s_tl.at[1])
    mate_load.start()
    mate_load.wait()

    def step_units(s):
        return [u for u in range(len(UNITS)) if UNITS[u][2] == s]

    for s in range(NB):
        side, cross, z_self, z_mate = step_units(s)
        d_copy[s].wait_recv()
        od_copy[s].start()
        a_copy0[s].wait_recv()
        oa_copy[s].start()

        fill(pan_d, far_table(1, 0), s, 0, 0)
        fill(pan_a, lambda b, t: far_smem[3, hi * 4 + b, t], s, 2, 0)
        turn(pan_a, lambda b, t: far_smem[3, hi * 4 + b, t], s, put_cross(s))
        u_copy[s].wait_recv()
        turn(pan_u, far_table(2, 1), s, put_left(1, s))
        od_copy[s].wait_recv()
        fill(pan_od, mate_table(1, 0), s, 0, 1)
        oa_copy[s].wait_recv()
        fill(pan_oa, lambda b, t: mate_smem[2, hi * 4 + b, t], s, 2, 1)

        upto, now = list(range(s + 1)), pl.ds(s * 256, 256)
        put_grid(cross, dot(cross_t[pl.ds(0, 128 * (s + 1)), :], dense[hi, :, now]), upto, [s])
        if s > 0:
            put_grid(cross, dot(cross_t[pl.ds(128 * s, 128), :], dense[hi, :, pl.ds(0, 256 * s)]),
                     [s], list(range(s)))
        send(cross)
        put_grid(side, dot(left[hi, pl.ds(0, 128 * (s + 1)), :], dense[2, :, now]), upto, [s])
        if s > 0:
            put_grid(side, dot(left[hi, pl.ds(128 * s, 128), :], dense[2, :, pl.ds(0, 256 * s)]),
                     [s], list(range(s)))
        send(side)
        down = dot(left[0, pl.ds(0, NB * 128), :], dense[0, :, now])
        up = dot(left[1, pl.ds(128 * s, 128), :], dense[1])
        for i in range(NB):
            for lane, u in enumerate((z_self, z_mate)):
                put(u, i, down[i * 128:(i + 1) * 128, lane * 128:(lane + 1) * 128])
                put(u, NB + i, up[:, i * 256 + lane * 128:i * 256 + (lane + 1) * 128])
        send(z_self)
        send(z_mate)
        if s == 0:
            for dy in range(1, NY):
                g_recv(dy).wait_recv()
            g_sum[...] = ((g_in[0] + g_in[1]) + g_in[2]) + g_in[3]
            gx_copy.start()
        for u in step_units(s - 1):
            y_finish(u)
        if s > 0:
            for u in step_units(s - 2):
                x_finish(u)
        if s > 1:
            for u in step_units(s - 3):
                fin_finish(u)

    gx_copy.wait_recv()
    for b in range(NB):
        at = pl.ds(b * 128, 128)
        grad[pl.ds(b, 1), :] = g_sum[pl.ds(0, 1), at] + g_x[pl.ds(0, 1), at]
    last = step_units(NB - 1)
    for u in step_units(NB - 2):
        x_finish(u)
    for u in last:
        y_finish(u)
    for u in step_units(NB - 3):
        fin_finish(u)
    for u in last:
        x_finish(u)
    for u in step_units(NB - 2) + last:
        fin_finish(u)
    for u in range(len(UNITS)):
        if UNITS[u][0] == "z":
            z_place(u)

    for cp in t_copy + [mt_copy] + d_copy + u_copy + a_copy0 + m_copy + od_copy + oa_copy:
        cp.wait_send()
    for u in range(len(UNITS)):
        kind = UNITS[u][0]

        def drain():
            for dy in range(1, NY):
                y_copy(u, dy).wait_send()
            xl_copy(u).wait_send()
            if kind == "side":
                pl.when(hi == 1)(lambda: fin_copy(u).wait_send())
            elif kind in ("cross", "z"):
                fin_copy(u).wait_send()

        on(u, drain)
    for dy in range(1, NY):
        g_copy(dy).wait_send()
    gx_copy.wait_send()


def on_device(jacobian_tiles, tip_lists, counts, residual):
    _, blocks, slots, tile, _ = jacobian_tiles.shape
    depth = residual.shape[1]
    rows = tile // lax.axis_size("freq")
    n = len(UNITS)
    width = blocks * tile
    dma = pltpu.SemaphoreType.DMA
    bf16, f32, i16, i32 = jnp.bfloat16, jnp.float32, jnp.int16, jnp.int32
    vm = pltpu.VMEM
    half = [vm((slots // 2 + 1, tile, tile), bf16)] * blocks
    coded = TOTAL * tile + n * NY * SCALE_ROWS
    per_block = [dma((blocks,))] * 2
    band, grad = pl.pallas_call(
        band_kernel,
        out_shape=(
            jax.ShapeDtypeStruct((blocks, SHIFTS + 1, blocks, rows, tile), f32),
            jax.ShapeDtypeStruct((blocks, tile), f32),
        ),
        in_specs=[
            pl.BlockSpec(memory_space=pltpu.HBM),
            pl.BlockSpec(memory_space=pltpu.SMEM),
            pl.BlockSpec(memory_space=pltpu.SMEM),
            pl.BlockSpec(memory_space=pltpu.HBM),
        ],
        out_specs=(pl.BlockSpec(memory_space=pltpu.VMEM), pl.BlockSpec(memory_space=pltpu.VMEM)),
        scratch_shapes=[
            [vm((slots, tile, tile), bf16)] * blocks, half, half, half, half, half, half, half, half, half,
            vm((1, depth), bf16), vm((2, 8, 128), i32), pltpu.SMEM((2, 8, 128), i32),
            vm((4, 8, 128), i32), pltpu.SMEM((4, 8, 128), i32),
            vm((3, 8, 128), i32), pltpu.SMEM((3, 8, 128), i32),
            vm((4, depth // 2, 2 * width), bf16), vm((2, width + 16, depth // 2), bf16),
            vm((width + 16, depth // 2), bf16), vm((width, depth // 2), bf16),
            vm((TOTAL * tile, tile), f32), vm((coded, tile), i16), vm((NY - 1, coded // NY, tile), i16),
            vm((TOTAL * 2 * rows, tile), f32), vm((TOTAL * rows, tile), f32),
            vm((TOTAL * rows, tile), f32), vm((TOTAL * rows, tile), f32),
            vm((8, width), f32), vm((NY, 8, width), f32), vm((8, width), f32), vm((8, width), f32),
            dma((blocks + 2,)), dma((5,)), dma((5,)), dma((2,)),
            *per_block, *per_block, *per_block, dma((2 * blocks,)), dma((2 * blocks,)),
            *per_block, *per_block,
            dma((n * (NY - 1),)), dma((n * (NY - 1),)), dma((n,)), dma((n,)), dma((n,)), dma((n,)),
            dma((NY,)), dma((NY,)),
        ],
        compiler_params=pltpu.CompilerParams(
            collective_id=0, has_side_effects=True, vmem_limit_bytes=63 * 1024 * 1024),
    )(jacobian_tiles.reshape(blocks, slots, tile, tile), tip_lists, counts, residual)
    return band, grad.reshape(width)


def solution(mesh):
    placed = (P("freq", "cells", None, None, None), P("cells", None), P("cells"), P("freq", None))
    return jax.shard_map(
        on_device,
        mesh=mesh,
        in_specs=placed,
        out_specs=(P("cells", None, None, "freq", None), P("cells")),
        check_vma=False,
    )
```

```python
import jax
import jax.numpy as jnp
from jax import lax
from jax.experimental import pallas as pl
from jax.experimental.pallas import tpu as pltpu
from jax.sharding import PartitionSpec as P

SHIFTS = 4
NY = 4
NB = 3
SCALE_ROWS = 16
MESH = pl.DeviceIdType.MESH


def unit_list():
    units = [
        ("own", None, -1, [(a, 0, b) for b in range(NB) for a in range(NB)]),
        ("mate", 0, -1, [(a, 1, b) for b in range(NB) for a in range(NB)]),
    ]
    for s in range(NB):
        grid = [(a, lane, s) for a in range(s + 1) for lane in range(2)]
        grid += [(s, lane, b) for b in range(s) for lane in range(2)]
        units.append(("side", None, s, grid))
        units.append(("cross", None, s, grid))
        for lane in range(2):
            down = [(a, lane, s) for a in range(NB)]
            up = [(s, lane, b) for b in range(NB)]
            units.append(("z", 1 if lane else None, s, down + up))
    return units


UNITS = unit_list()
COUNT = [len(blocks) for _, _, _, blocks in UNITS]
BASE = [sum(COUNT[:u]) for u in range(len(UNITS))]
TOTAL = sum(COUNT)


def band_kernel(
    jac, tip_lists, counts, resid_hbm, band, grad,
    raw, pk0, pk1, turned0, turned1, mate0, mate1, pan_d, pan_od, pan_u, pan_a, pan_oa, turned_a,
    resid, tab, tab_smem, far_tab, far_smem, mate_tab, mate_smem,
    dense, left, odd_t, cross_t, prod, coded, y_in, y_sum, fin_in, scale,
    g_own, g_in, g_sum, g_x,
    s_load, s_ts, s_tr, s_tl, s_ds, s_dr, s_us, s_ur, s_as, s_ar, s_ms, s_mr,
    s_ods, s_odr, s_oas, s_oar, s_ys, s_yr, s_fs, s_fr, s_gs, s_gr,
):
    slots = jac.shape[1]
    half = slots // 2
    pairs = resid_hbm.shape[1] // 256
    rows = band.shape[3]
    f = lax.axis_index("freq")
    d = lax.axis_index("cells")
    nf = lax.axis_size("freq")
    nd = lax.axis_size("cells")
    y, xl = f // 2, lax.rem(f, 2)
    hi, core = lax.rem(d // 2, 2), lax.rem(d, 2)

    def ydev(dy):
        return (lax.rem(f + 2 * dy, nf), d)

    below = (f, lax.rem(d - 4 + nd, nd))
    above = (f, lax.rem(d + 4, nd))
    x_pair = (f, d + 2 - 4 * hi)
    core_pair = (f, d + 1 - 2 * core)
    twin = f + 1 - 2 * xl
    xl_pair = (twin, d)

    loads = []
    for b in range(NB):
        loads.append(pltpu.make_async_copy(jac.at[b], raw[b], s_load.at[b]))
    loads.append(pltpu.make_async_copy(resid_hbm, resid, s_load.at[NB]))
    for cp in loads:
        cp.start()

    barrier = pltpu.get_barrier_semaphore()
    partners = [below, above, x_pair, core_pair] + [ydev(dy) for dy in range(1, NY)]
    partners += [xl_pair, (twin, below[1]), (twin, above[1]), (twin, x_pair[1])]
    for dev in partners:
        pl.semaphore_signal(barrier, inc=1, device_id=dev, device_id_type=MESH)

    row = lax.broadcasted_iota(jnp.int32, (8, 128), 0)
    col = lax.broadcasted_iota(jnp.int32, (8, 128), 1)
    place = jnp.full((8, 128), half, jnp.int32)
    slot = jnp.zeros((8, 128), jnp.int32)
    for b in range(NB):
        odd_before = 0
        for p in range(slots):
            name = tip_lists[b, p]
            parity = lax.rem(name, 2)
            rank = jnp.where(parity == 1, odd_before, p - odd_before)
            odd_before = odd_before + parity
            mine = row == parity * 4 + b
            slot = jnp.where(mine & (col == rank), p, slot)
            named = jnp.where(p < counts[b], name // 2, -1)
            place = jnp.where(mine & (col == named), rank, place)
    tab[0] = place
    tab[1] = slot
    own_tab = pltpu.make_async_copy(tab, tab_smem, s_load.at[NB + 1])
    own_tab.start()
    zero = jnp.zeros((128, 128), jnp.bfloat16)
    for panel in (pk0, pk1, turned0, turned1, mate0, mate1,
                  pan_d, pan_od, pan_u, pan_a, pan_oa, turned_a):
        for block in panel:
            block[half] = zero
    for cp in loads:
        cp.wait()
    own_tab.wait()

    def pack(b):
        def step(i, carry):
            even, odd = raw[b][tab_smem[1, b, i]], raw[b][tab_smem[1, 4 + b, i]]
            pk0[b][i], pk1[b][i] = even, odd
            turned0[b][i], turned1[b][i] = even.T, odd.T
            return carry

        lax.fori_loop(0, half, step, 0, unroll=2)

    pack(0)
    pl.semaphore_wait(barrier, len(partners))

    def remote(src, dst, ss, rs, dev):
        return pltpu.make_async_remote_copy(
            src_ref=src, dst_ref=dst, send_sem=ss, recv_sem=rs,
            device_id=dev, device_id_type=MESH)

    live = pl.ds(0, half)

    def panel_copies(src, dst, ss, rs, dev, first=0):
        return [
            remote(src[b].at[live], dst[b].at[live], ss.at[first + b], rs.at[first + b], dev)
            for b in range(NB)]

    d_copy = panel_copies(pk0, pan_d, s_ds, s_dr, below)
    u_copy = panel_copies(turned1, pan_u, s_us, s_ur, above)
    a_copy0 = panel_copies(pk0, pan_a, s_as, s_ar, x_pair)
    a_copy1 = panel_copies(pk1, pan_a, s_as, s_ar, x_pair)
    m_copy = panel_copies(pk0, mate0, s_ms, s_mr, core_pair)
    m_copy += panel_copies(pk1, mate1, s_ms, s_mr, core_pair, NB)
    od_copy = panel_copies(pan_d, pan_od, s_ods, s_odr, core_pair)
    oa_copy = panel_copies(pan_a, pan_oa, s_oas, s_oar, core_pair)
    t_copy = [
        remote(tab.at[0], far_tab.at[i], s_ts.at[i], s_tr.at[i], dev)
        for i, dev in enumerate((core_pair, below, above, x_pair))]
    mt_copy = remote(far_tab.at[pl.ds(1, 3)], mate_tab, s_ts.at[4], s_tr.at[4], core_pair)

    for b in range(NB):
        if b > 0:
            pack(b)
        d_copy[b].start()
        u_copy[b].start()

        @pl.when(hi == 1)
        def _():
            a_copy0[b].start()

        @pl.when(hi == 0)
        def _():
            a_copy1[b].start()

        if b == 0:
            for cp in t_copy:
                cp.start()
        m_copy[b].start()
        m_copy[NB + b].start()

    def turn(panel, table, b, put_tile):
        def step(t, carry):
            at = pl.ds(pl.multiple_of(t * 128, 128), 128)
            put_tile(at, panel[b][table(b, t)])
            return carry

        lax.fori_loop(0, pairs, step, 0, unroll=4)

    def fill(panel, table, b, which, lane):
        at = pl.ds(b * 256 + lane * 128, 128)

        def step(t, carry):
            dense[which, pl.ds(pl.multiple_of(t * 128, 128), 128), at] = panel[b][table(b, t)]
            return carry

        lax.fori_loop(0, pairs, step, 0, unroll=4)

    def own_table(parity):
        return lambda b, t: tab_smem[0, parity * 4 + b, t]

    def far_table(i, parity):
        return lambda b, t: far_smem[i, parity * 4 + b, t]

    def mate_table(i, parity):
        return lambda b, t: mate_smem[i - 1, parity * 4 + b, t]

    def put_left(which, b):
        def put(at, tile):
            left[which, pl.ds(b * 128, 128), at] = tile
        return put

    def put_odd(b):
        def put(at, tile):
            odd_t[pl.ds(b * 128, 128), at] = tile
        return put

    def put_cross(b):
        def put(at, tile):
            cross_t[pl.ds(b * 128, 128), at] = tile
        return put

    below_rows = pl.ds(NB * 128, 16)
    for t in range(pairs):
        at = pl.ds(t * 128, 128)
        left[0, below_rows, at] = jnp.broadcast_to(resid[:, pl.ds(t * 256, 128)], (16, 128))
        odd_t[below_rows, at] = jnp.broadcast_to(resid[:, pl.ds(t * 256 + 128, 128)], (16, 128))
    for b in range(NB):
        turn(turned0, own_table(0), b, put_left(0, b))
        turn(turned1, own_table(1), b, put_odd(b))
        fill(pk0, own_table(0), b, 3, 0)
        fill(pk1, own_table(1), b, 1, 0)

    for cp in t_copy:
        cp.wait_recv()
    mt_copy.start()
    far_load = pltpu.make_async_copy(far_tab, far_smem, s_tl.at[0])
    far_load.start()
    far_load.wait()

    def on(u, body):
        which = UNITS[u][1]
        if which is None:
            body()
        else:
            pl.when(core == which)(body)

    def coded_base(u):
        return BASE[u] * 128 + u * NY * SCALE_ROWS

    def y_part(u):
        return COUNT[u] * 2 * rows + SCALE_ROWS

    def y_copy(u, dy):
        part = y_part(u)
        take = pl.ds(pl.multiple_of(coded_base(u) + lax.rem(y + dy, NY) * part, 16), part)
        i = u * (NY - 1) + dy - 1
        return remote(coded.at[take], y_in.at[dy - 1, pl.ds(coded_base(u) // NY, part)],
                      s_ys.at[i], s_yr.at[i], ydev(dy))

    def sums(u, half_of, first, n):
        at = BASE[u] * 2 * rows + half_of * COUNT[u] * rows + first * rows
        return pl.ds(pl.multiple_of(at, 8), n * rows)

    def landed(u, first, n):
        return pl.ds((BASE[u] + first) * rows, n * rows)

    def owner_copies(u):
        kind, n = UNITS[u][0], COUNT[u]

        def copy(i, from_other, first, n, dev):
            src = y_sum.at[sums(u, 1 - xl if from_other else xl, first, n)]
            return remote(src, fin_in.at[from_other, landed(u, first, n)],
                          s_fs.at[3 * u + i], s_fr.at[3 * u + i], dev)

        if kind == "side":
            owner = lax.rem(d - 4 * hi + nd, nd)
            return [(None, copy(1, 1, 0, n, (twin, owner))), (1, copy(0, 0, 0, n, below))]
        if kind == "cross":
            return [(None, copy(1, 1, 0, n, (twin, x_pair[1]))), (None, copy(0, 0, 0, n, x_pair))]
        if kind == "z":
            return [(None, copy(2, 1, 0, NB, xl_pair)),
                    (None, copy(1, 1, NB, NB, (twin, below[1]))), (None, copy(0, 0, NB, NB, below))]
        return [(None, copy(1, 1, 0, n, xl_pair))]

    def each(u, act):
        for side_of, cp in owner_copies(u):
            if side_of is None:
                act(cp)
            else:
                pl.when(hi == side_of)(lambda: act(cp))

    line = lax.broadcasted_iota(jnp.int32, (SCALE_ROWS, 128), 0)

    def send(u):
        n = COUNT[u]

        def body():
            parts = [lax.rem(y + dy, NY) for dy in range(1, NY)]

            def code(i, powers):
                new = []
                for part, known in zip(parts, powers):
                    src = pl.multiple_of(BASE[u] * 128 + part * n * 32 + i * 32, 32)
                    dst = pl.multiple_of(coded_base(u) + part * y_part(u) + i * 32, 16)
                    value = prod[pl.ds(src, 32)]
                    top = jnp.maximum(jnp.max(jnp.abs(value), axis=0, keepdims=True), 1e-33)
                    power = jnp.ceil(jnp.log2(top) + 1e-3)
                    up = jnp.exp2(15.0 - power) * (32766.0 / 32768.0)
                    coded[pl.ds(dst, 32)] = jnp.round(value * up).astype(jnp.int32).astype(jnp.int16)
                    new.append(jnp.where(line == i, power, known))
                return tuple(new)

            powers = lax.fori_loop(0, n, code, (jnp.zeros((SCALE_ROWS, 128), jnp.float32),) * (NY - 1))
            for part, power in zip(parts, powers):
                dst = pl.multiple_of(coded_base(u) + part * y_part(u) + n * 32, 16)
                coded[pl.ds(dst, SCALE_ROWS)] = power.astype(jnp.int32).astype(jnp.int16)
            for dy in range(1, NY):
                y_copy(u, dy).start()

        on(u, body)

    def y_finish(u):
        n = COUNT[u]

        def body():
            for dy in range(1, NY):
                y_copy(u, dy).wait_recv()
                power = y_in[dy - 1, pl.ds(coded_base(u) // NY + n * 32, SCALE_ROWS)]
                power = power.astype(jnp.int32).astype(jnp.float32)
                scale[dy - 1] = jnp.exp2(power - 15.0) * (32768.0 / 32766.0)

            def step(i, carry):
                at = pl.ds(pl.multiple_of(BASE[u] * 128 + y * n * 32 + i * 32, 32), 32)
                total = prod[at]
                for dy in range(1, NY):
                    src = pl.ds(pl.multiple_of(coded_base(u) // NY + i * 32, 16), 32)
                    part = y_in[dy - 1, src].astype(jnp.int32).astype(jnp.float32)
                    total = total + part * scale[dy - 1, pl.ds(i, 1)]
                y_sum[pl.ds(pl.multiple_of(BASE[u] * 32 + i * 32, 32), 32)] = total
                return carry

            lax.fori_loop(0, n, step, 0)
            each(u, lambda cp: cp.start())

        on(u, body)

    def here(u, i):
        return y_sum[sums(u, xl, i, 1)] + fin_in[1, landed(u, i, 1)]

    def arrived(u, i):
        return fin_in[0, landed(u, i, 1)] + fin_in[1, landed(u, i, 1)]

    def fin_finish(u):
        kind, _, _, blocks = UNITS[u]

        def body():
            each(u, lambda cp: cp.wait_recv())
            if kind in ("own", "mate"):
                for i, (a, lane, b) in enumerate(blocks):
                    band[a, lane, b] = here(u, i)
            elif kind == "side":
                for side_of, value in ((0, here), (1, arrived)):
                    @pl.when(hi == side_of)
                    def _():
                        for i, (a, lane, b) in enumerate(blocks):
                            band[a, 3 - 2 * core if lane else 2, b] = value(u, i)
            elif kind == "cross":
                for i, (a, lane, b) in enumerate(blocks):
                    k = 3 - 2 * core if lane else 2
                    band[a, k, b] = band[a, k, b] + arrived(u, i)

        on(u, body)

    z_down = {block: (u, i) for u in range(len(UNITS)) if UNITS[u][0] == "z"
              for i, block in enumerate(UNITS[u][3][:NB])}

    def z_place(u):
        def body():
            for i, (a, lane, b) in enumerate(UNITS[u][3][NB:]):
                band[a, 3 if lane else 4, b] = here(*z_down[(a, lane, b)]) + arrived(u, NB + i)

        on(u, body)

    def put(u, i, block):
        for g in range(2 * NY):
            at = pl.ds(BASE[u] * 128 + (g * COUNT[u] + i) * rows, rows)
            prod[at] = block[g * rows:(g + 1) * rows]

    def put_grid(u, out, rows_of, cols_of):
        for i, (a, lane, b) in enumerate(UNITS[u][3]):
            if a in rows_of and b in cols_of:
                r, c = rows_of.index(a) * 128, cols_of.index(b) * 256 + lane * 128
                put(u, i, out[r:r + 128, c:c + 128])

    def dot(a, b):
        return jnp.dot(a, b, preferred_element_type=jnp.float32)

    for b in range(NB):
        m_copy[b].wait_recv()
        m_copy[NB + b].wait_recv()
        fill(mate0, far_table(0, 0), b, 3, 1)
        fill(mate1, far_table(0, 1), b, 1, 1)
        at = pl.ds(b * 256, 256)
        out = dot(left[0], dense[3, :, at]) + dot(odd_t[...], dense[1, :, at])
        for a in range(NB):
            put(0, b * NB + a, out[a * 128:(a + 1) * 128, :128])
            put(1, b * NB + a, out[a * 128:(a + 1) * 128, 128:])
        g_own[:, pl.ds(b * 128, 128)] = out[NB * 128:NB * 128 + 8, :128]
    send(0)
    send(1)

    def g_copy(dy):
        return remote(g_own, g_in.at[y], s_gs.at[dy - 1], s_gr.at[dy - 1], ydev(dy))

    def g_recv(dy):
        return remote(g_own, g_in.at[lax.rem(y - dy + NY, NY)], s_gs.at[dy - 1], s_gr.at[dy - 1], ydev(dy))

    gx_copy = remote(g_sum, g_x, s_gs.at[NY - 1], s_gr.at[NY - 1], xl_pair)
    for dy in range(1, NY):
        g_copy(dy).start()
    g_in[y] = g_own[...]

    mt_copy.wait_recv()
    mate_load = pltpu.make_async_copy(mate_tab, mate_smem, s_tl.at[1])
    mate_load.start()
    mate_load.wait()

    def step_units(s):
        return [u for u in range(len(UNITS)) if UNITS[u][2] == s]

    for s in range(NB):
        side, cross, z_self, z_mate = step_units(s)
        d_copy[s].wait_recv()
        od_copy[s].start()
        a_copy0[s].wait_recv()
        oa_copy[s].start()

        fill(pan_d, far_table(1, 0), s, 0, 0)
        fill(pan_a, lambda b, t: far_smem[3, hi * 4 + b, t], s, 2, 0)

        def turn_tile(i, carry):
            turned_a[s][i] = pan_a[s][i].T
            return carry

        lax.fori_loop(0, half, turn_tile, 0, unroll=2)
        turn(turned_a, lambda b, t: far_smem[3, hi * 4 + b, t], s, put_cross(s))
        u_copy[s].wait_recv()
        turn(pan_u, far_table(2, 1), s, put_left(1, s))
        od_copy[s].wait_recv()
        fill(pan_od, mate_table(1, 0), s, 0, 1)
        oa_copy[s].wait_recv()
        fill(pan_oa, lambda b, t: mate_smem[2, hi * 4 + b, t], s, 2, 1)

        upto, now = list(range(s + 1)), pl.ds(s * 256, 256)
        put_grid(cross, dot(cross_t[pl.ds(0, 128 * (s + 1)), :], dense[hi, :, now]), upto, [s])
        if s > 0:
            put_grid(cross, dot(cross_t[pl.ds(128 * s, 128), :], dense[hi, :, pl.ds(0, 256 * s)]),
                     [s], list(range(s)))
        send(cross)
        put_grid(side, dot(left[hi, pl.ds(0, 128 * (s + 1)), :], dense[2, :, now]), upto, [s])
        if s > 0:
            put_grid(side, dot(left[hi, pl.ds(128 * s, 128), :], dense[2, :, pl.ds(0, 256 * s)]),
                     [s], list(range(s)))
        send(side)
        down = dot(left[0, pl.ds(0, NB * 128), :], dense[0, :, now])
        up = dot(left[1, pl.ds(128 * s, 128), :], dense[1])
        for i in range(NB):
            for lane, u in enumerate((z_self, z_mate)):
                put(u, i, down[i * 128:(i + 1) * 128, lane * 128:(lane + 1) * 128])
                put(u, NB + i, up[:, i * 256 + lane * 128:i * 256 + (lane + 1) * 128])
        send(z_self)
        send(z_mate)
        if s == 0:
            for dy in range(1, NY):
                g_recv(dy).wait_recv()
            g_sum[...] = ((g_in[0] + g_in[1]) + g_in[2]) + g_in[3]
            gx_copy.start()
        for u in step_units(s - 1):
            y_finish(u)
        if s > 0:
            for u in step_units(s - 2):
                fin_finish(u)

    gx_copy.wait_recv()
    for b in range(NB):
        at = pl.ds(b * 128, 128)
        grad[pl.ds(b, 1), :] = g_sum[pl.ds(0, 1), at] + g_x[pl.ds(0, 1), at]
    for u in step_units(NB - 1):
        y_finish(u)
    for u in step_units(NB - 2) + step_units(NB - 1):
        fin_finish(u)
    for u in range(len(UNITS)):
        if UNITS[u][0] == "z":
            z_place(u)

    for cp in t_copy + [mt_copy] + d_copy + u_copy + a_copy0 + m_copy + od_copy + oa_copy:
        cp.wait_send()
    for u in range(len(UNITS)):
        def drain():
            for dy in range(1, NY):
                y_copy(u, dy).wait_send()
            each(u, lambda cp: cp.wait_send())

        on(u, drain)
    for dy in range(1, NY):
        g_copy(dy).wait_send()
    gx_copy.wait_send()


def on_device(jacobian_tiles, tip_lists, counts, residual):
    _, blocks, slots, tile, _ = jacobian_tiles.shape
    depth = residual.shape[1]
    rows = tile // lax.axis_size("freq")
    n = len(UNITS)
    width = blocks * tile
    dma = pltpu.SemaphoreType.DMA
    bf16, f32, i16, i32 = jnp.bfloat16, jnp.float32, jnp.int16, jnp.int32
    vm = pltpu.VMEM
    half = [vm((slots // 2 + 1, tile, tile), bf16)] * blocks
    coded = TOTAL * tile + n * NY * SCALE_ROWS
    per_block = [dma((blocks,))] * 2
    band, grad = pl.pallas_call(
        band_kernel,
        out_shape=(
            jax.ShapeDtypeStruct((blocks, SHIFTS + 1, blocks, rows, tile), f32),
            jax.ShapeDtypeStruct((blocks, tile), f32),
        ),
        in_specs=[
            pl.BlockSpec(memory_space=pltpu.HBM),
            pl.BlockSpec(memory_space=pltpu.SMEM),
            pl.BlockSpec(memory_space=pltpu.SMEM),
            pl.BlockSpec(memory_space=pltpu.HBM),
        ],
        out_specs=(pl.BlockSpec(memory_space=pltpu.VMEM), pl.BlockSpec(memory_space=pltpu.VMEM)),
        scratch_shapes=[
            [vm((slots, tile, tile), bf16)] * blocks, *[half] * 12,
            vm((1, depth), bf16), vm((2, 8, 128), i32), pltpu.SMEM((2, 8, 128), i32),
            vm((4, 8, 128), i32), pltpu.SMEM((4, 8, 128), i32),
            vm((3, 8, 128), i32), pltpu.SMEM((3, 8, 128), i32),
            vm((4, depth // 2, 2 * width), bf16), vm((2, width + 16, depth // 2), bf16),
            vm((width + 16, depth // 2), bf16), vm((width, depth // 2), bf16),
            vm((TOTAL * tile, tile), f32), vm((coded, tile), i16), vm((NY - 1, coded // NY, tile), i16),
            vm((TOTAL * 2 * rows, tile), f32), vm((2, TOTAL * rows, tile), f32),
            vm((NY - 1, SCALE_ROWS, tile), f32),
            vm((8, width), f32), vm((NY, 8, width), f32), vm((8, width), f32), vm((8, width), f32),
            dma((blocks + 2,)), dma((5,)), dma((5,)), dma((2,)),
            *per_block, *per_block, *per_block, dma((2 * blocks,)), dma((2 * blocks,)),
            *per_block, *per_block,
            dma((n * (NY - 1),)), dma((n * (NY - 1),)), dma((3 * n,)), dma((3 * n,)),
            dma((NY,)), dma((NY,)),
        ],
        compiler_params=pltpu.CompilerParams(
            collective_id=0, has_side_effects=True, vmem_limit_bytes=63 * 1024 * 1024),
    )(jacobian_tiles.reshape(blocks, slots, tile, tile), tip_lists, counts, residual)
    return band, grad.reshape(width)


def solution(mesh):
    placed = (P("freq", "cells", None, None, None), P("cells", None), P("cells"), P("freq", None))
    return jax.shard_map(
        on_device,
        mesh=mesh,
        in_specs=placed,
        out_specs=(P("cells", None, None, "freq", None), P("cells")),
        check_vma=False,
    )
```

```python
import jax
import jax.numpy as jnp
from jax import lax
from jax.experimental import pallas as pl
from jax.experimental.pallas import tpu as pltpu
from jax.sharding import PartitionSpec as P

SHIFTS = 4
NY = 4
NB = 3
SCALE_ROWS = 16
MESH = pl.DeviceIdType.MESH


def unit_list():
    units = [
        ("own", None, -1, [(a, 0, b) for b in range(NB) for a in range(NB)]),
        ("mate", 0, -1, [(a, 1, b) for b in range(NB) for a in range(NB)]),
    ]
    for s in range(NB):
        grid = [(a, lane, s) for a in range(s + 1) for lane in range(2)]
        grid += [(s, lane, b) for b in range(s) for lane in range(2)]
        units.append(("side", None, s, grid))
        units.append(("cross", None, s, grid))
        for lane in range(2):
            down = [(a, lane, s) for a in range(NB)]
            up = [(s, lane, b) for b in range(NB)]
            units.append(("z", 1 if lane else None, s, down + up))
    return units


UNITS = unit_list()
COUNT = [len(blocks) for _, _, _, blocks in UNITS]
BASE = [sum(COUNT[:u]) for u in range(len(UNITS))]
TOTAL = sum(COUNT)


def band_kernel(
    jac, tip_lists, counts, resid_hbm, band, grad,
    raw, pk0, pk1, turned0, turned1, mate0, mate1, pan_d, pan_od, pan_u, pan_a, pan_oa, turned_a,
    resid, tab, tab_smem, far_tab, far_smem, mate_tab, mate_smem,
    dense, alone, left, odd_t, cross_t, prod, coded, y_in, y_sum, fin_in, scale,
    g_own, g_in, g_sum, g_x,
    s_load, s_ts, s_tr, s_tl, s_ds, s_dr, s_us, s_ur, s_as, s_ar, s_ms, s_mr,
    s_ods, s_odr, s_oas, s_oar, s_ys, s_yr, s_fs, s_fr, s_gs, s_gr,
):
    slots = jac.shape[1]
    half = slots // 2
    pairs = resid_hbm.shape[1] // 256
    rows = band.shape[3]
    f = lax.axis_index("freq")
    d = lax.axis_index("cells")
    nf = lax.axis_size("freq")
    nd = lax.axis_size("cells")
    y, xl = f // 2, lax.rem(f, 2)
    hi, core = lax.rem(d // 2, 2), lax.rem(d, 2)

    def ydev(dy):
        return (lax.rem(f + 2 * dy, nf), d)

    below = (f, lax.rem(d - 4 + nd, nd))
    above = (f, lax.rem(d + 4, nd))
    x_pair = (f, d + 2 - 4 * hi)
    core_pair = (f, d + 1 - 2 * core)
    twin = f + 1 - 2 * xl
    xl_pair = (twin, d)

    loads = []
    for b in range(NB):
        loads.append(pltpu.make_async_copy(jac.at[b], raw[b], s_load.at[b]))
    loads.append(pltpu.make_async_copy(resid_hbm, resid, s_load.at[NB]))
    for cp in loads:
        cp.start()

    barrier = pltpu.get_barrier_semaphore()
    partners = [below, above, x_pair, core_pair] + [ydev(dy) for dy in range(1, NY)]
    partners += [xl_pair, (twin, below[1]), (twin, above[1]), (twin, x_pair[1])]
    for dev in partners:
        pl.semaphore_signal(barrier, inc=1, device_id=dev, device_id_type=MESH)

    row = lax.broadcasted_iota(jnp.int32, (8, 128), 0)
    col = lax.broadcasted_iota(jnp.int32, (8, 128), 1)
    place = jnp.full((8, 128), half, jnp.int32)
    slot = jnp.zeros((8, 128), jnp.int32)
    for b in range(NB):
        odd_before = 0
        for p in range(slots):
            name = tip_lists[b, p]
            parity = lax.rem(name, 2)
            rank = jnp.where(parity == 1, odd_before, p - odd_before)
            odd_before = odd_before + parity
            mine = row == parity * 4 + b
            slot = jnp.where(mine & (col == rank), p, slot)
            named = jnp.where(p < counts[b], name // 2, -1)
            place = jnp.where(mine & (col == named), rank, place)
    tab[0] = place
    tab[1] = slot
    own_tab = pltpu.make_async_copy(tab, tab_smem, s_load.at[NB + 1])
    own_tab.start()
    zero = jnp.zeros((128, 128), jnp.bfloat16)
    for panel in (pk0, pk1, turned0, turned1, mate0, mate1,
                  pan_d, pan_od, pan_u, pan_a, pan_oa, turned_a):
        for block in panel:
            block[half] = zero
    for cp in loads:
        cp.wait()
    own_tab.wait()

    def pack(b):
        def step(i, carry):
            even, odd = raw[b][tab_smem[1, b, i]], raw[b][tab_smem[1, 4 + b, i]]
            pk0[b][i], pk1[b][i] = even, odd
            turned0[b][i], turned1[b][i] = even.T, odd.T
            return carry

        lax.fori_loop(0, half, step, 0, unroll=2)

    pack(0)
    pl.semaphore_wait(barrier, len(partners))

    def remote(src, dst, ss, rs, dev):
        return pltpu.make_async_remote_copy(
            src_ref=src, dst_ref=dst, send_sem=ss, recv_sem=rs,
            device_id=dev, device_id_type=MESH)

    live = pl.ds(0, half)

    def panel_copies(src, dst, ss, rs, dev, first=0):
        return [
            remote(src[b].at[live], dst[b].at[live], ss.at[first + b], rs.at[first + b], dev)
            for b in range(NB)]

    d_copy = panel_copies(pk0, pan_d, s_ds, s_dr, below)
    u_copy = panel_copies(turned1, pan_u, s_us, s_ur, above)
    a_copy0 = panel_copies(pk0, pan_a, s_as, s_ar, x_pair)
    a_copy1 = panel_copies(pk1, pan_a, s_as, s_ar, x_pair)
    m_copy = panel_copies(pk0, mate0, s_ms, s_mr, core_pair)
    m_copy += panel_copies(pk1, mate1, s_ms, s_mr, core_pair, NB)
    od_copy = panel_copies(pan_d, pan_od, s_ods, s_odr, core_pair)
    oa_copy = panel_copies(pan_a, pan_oa, s_oas, s_oar, core_pair)
    t_copy = [
        remote(tab.at[0], far_tab.at[i], s_ts.at[i], s_tr.at[i], dev)
        for i, dev in enumerate((core_pair, below, above, x_pair))]
    mt_copy = remote(far_tab.at[pl.ds(1, 3)], mate_tab, s_ts.at[4], s_tr.at[4], core_pair)

    for b in range(NB):
        if b > 0:
            pack(b)
        d_copy[b].start()
        u_copy[b].start()

        @pl.when(hi == 1)
        def _():
            a_copy0[b].start()

        @pl.when(hi == 0)
        def _():
            a_copy1[b].start()

        if b == 0:
            for cp in t_copy:
                cp.start()
        m_copy[b].start()
        m_copy[NB + b].start()

    def turn(panel, table, b, put_tile):
        def step(t, carry):
            at = pl.ds(pl.multiple_of(t * 128, 128), 128)
            put_tile(at, panel[b][table(b, t)])
            return carry

        lax.fori_loop(0, pairs, step, 0, unroll=4)

    def fill(panel, table, b, which, lane):
        at = pl.ds(b * 256 + lane * 128, 128)

        def step(t, carry):
            dense[which, pl.ds(pl.multiple_of(t * 128, 128), 128), at] = panel[b][table(b, t)]
            return carry

        lax.fori_loop(0, pairs, step, 0, unroll=4)

    def fill_alone(panel, table, b, parity):
        at = pl.ds(b * 128, 128)

        def step(t, carry):
            alone[parity, pl.ds(pl.multiple_of(t * 128, 128), 128), at] = panel[b][table(b, t)]
            return carry

        lax.fori_loop(0, pairs, step, 0, unroll=4)

    def own_table(parity):
        return lambda b, t: tab_smem[0, parity * 4 + b, t]

    def far_table(i, parity):
        return lambda b, t: far_smem[i, parity * 4 + b, t]

    def mate_table(i, parity):
        return lambda b, t: mate_smem[i - 1, parity * 4 + b, t]

    def put_left(which, b):
        def put(at, tile):
            left[which, pl.ds(b * 128, 128), at] = tile
        return put

    def put_odd(b):
        def put(at, tile):
            odd_t[pl.ds(b * 128, 128), at] = tile
        return put

    def put_cross(b):
        def put(at, tile):
            cross_t[pl.ds(b * 128, 128), at] = tile
        return put

    below_rows = pl.ds(NB * 128, 16)
    for t in range(pairs):
        at = pl.ds(t * 128, 128)
        left[0, below_rows, at] = jnp.broadcast_to(resid[:, pl.ds(t * 256, 128)], (16, 128))
        odd_t[below_rows, at] = jnp.broadcast_to(resid[:, pl.ds(t * 256 + 128, 128)], (16, 128))
    for b in range(NB):
        turn(turned0, own_table(0), b, put_left(0, b))
        turn(turned1, own_table(1), b, put_odd(b))
        fill_alone(pk0, own_table(0), b, 0)
        fill_alone(pk1, own_table(1), b, 1)

    def on(u, body):
        which = UNITS[u][1]
        if which is None:
            body()
        else:
            pl.when(core == which)(body)

    def coded_base(u):
        return BASE[u] * 128 + u * NY * SCALE_ROWS

    def y_part(u):
        return COUNT[u] * 2 * rows + SCALE_ROWS

    def y_copy(u, dy):
        part = y_part(u)
        take = pl.ds(pl.multiple_of(coded_base(u) + lax.rem(y + dy, NY) * part, 16), part)
        i = u * (NY - 1) + dy - 1
        return remote(coded.at[take], y_in.at[dy - 1, pl.ds(coded_base(u) // NY, part)],
                      s_ys.at[i], s_yr.at[i], ydev(dy))

    def sums(u, half_of, first, n):
        at = BASE[u] * 2 * rows + half_of * COUNT[u] * rows + first * rows
        return pl.ds(pl.multiple_of(at, 8), n * rows)

    def landed(u, first, n):
        return pl.ds((BASE[u] + first) * rows, n * rows)

    def owner_copies(u):
        kind, n = UNITS[u][0], COUNT[u]

        def copy(i, from_other, first, n, dev):
            src = y_sum.at[sums(u, 1 - xl if from_other else xl, first, n)]
            return remote(src, fin_in.at[from_other, landed(u, first, n)],
                          s_fs.at[3 * u + i], s_fr.at[3 * u + i], dev)

        if kind == "side":
            owner = lax.rem(d - 4 * hi + nd, nd)
            return [(None, copy(1, 1, 0, n, (twin, owner))), (1, copy(0, 0, 0, n, below))]
        if kind == "cross":
            return [(None, copy(1, 1, 0, n, (twin, x_pair[1]))), (None, copy(0, 0, 0, n, x_pair))]
        if kind == "z":
            return [(None, copy(2, 1, 0, NB, xl_pair)),
                    (None, copy(1, 1, NB, NB, (twin, below[1]))), (None, copy(0, 0, NB, NB, below))]
        return [(None, copy(1, 1, 0, n, xl_pair))]

    def each(u, act):
        for side_of, cp in owner_copies(u):
            if side_of is None:
                act(cp)
            else:
                pl.when(hi == side_of)(lambda: act(cp))

    line = lax.broadcasted_iota(jnp.int32, (SCALE_ROWS, 128), 0)

    def send(u):
        n = COUNT[u]

        def body():
            parts = [lax.rem(y + dy, NY) for dy in range(1, NY)]

            def code(i, powers):
                new = []
                for part, known in zip(parts, powers):
                    src = pl.multiple_of(BASE[u] * 128 + part * n * 32 + i * 32, 32)
                    dst = pl.multiple_of(coded_base(u) + part * y_part(u) + i * 32, 16)
                    value = prod[pl.ds(src, 32)]
                    top = jnp.maximum(jnp.max(jnp.abs(value), axis=0, keepdims=True), 1e-33)
                    power = jnp.ceil(jnp.log2(top) + 1e-3)
                    up = jnp.exp2(15.0 - power) * (32766.0 / 32768.0)
                    coded[pl.ds(dst, 32)] = jnp.round(value * up).astype(jnp.int32).astype(jnp.int16)
                    new.append(jnp.where(line == i, power, known))
                return tuple(new)

            powers = lax.fori_loop(0, n, code, (jnp.zeros((SCALE_ROWS, 128), jnp.float32),) * (NY - 1))
            for part, power in zip(parts, powers):
                dst = pl.multiple_of(coded_base(u) + part * y_part(u) + n * 32, 16)
                coded[pl.ds(dst, SCALE_ROWS)] = power.astype(jnp.int32).astype(jnp.int16)
            for dy in range(1, NY):
                y_copy(u, dy).start()

        on(u, body)

    def y_finish(u):
        n = COUNT[u]

        def body():
            for dy in range(1, NY):
                y_copy(u, dy).wait_recv()
                power = y_in[dy - 1, pl.ds(coded_base(u) // NY + n * 32, SCALE_ROWS)]
                power = power.astype(jnp.int32).astype(jnp.float32)
                scale[dy - 1] = jnp.exp2(power - 15.0) * (32768.0 / 32766.0)

            def step(i, carry):
                at = pl.ds(pl.multiple_of(BASE[u] * 128 + y * n * 32 + i * 32, 32), 32)
                total = prod[at]
                for dy in range(1, NY):
                    src = pl.ds(pl.multiple_of(coded_base(u) // NY + i * 32, 16), 32)
                    part = y_in[dy - 1, src].astype(jnp.int32).astype(jnp.float32)
                    total = total + part * scale[dy - 1, pl.ds(i, 1)]
                y_sum[pl.ds(pl.multiple_of(BASE[u] * 32 + i * 32, 32), 32)] = total
                return carry

            lax.fori_loop(0, n, step, 0)
            each(u, lambda cp: cp.start())

        on(u, body)

    def here(u, i):
        return y_sum[sums(u, xl, i, 1)] + fin_in[1, landed(u, i, 1)]

    def arrived(u, i):
        return fin_in[0, landed(u, i, 1)] + fin_in[1, landed(u, i, 1)]

    def fin_finish(u):
        kind, _, _, blocks = UNITS[u]

        def body():
            each(u, lambda cp: cp.wait_recv())
            if kind in ("own", "mate"):
                for i, (a, lane, b) in enumerate(blocks):
                    band[a, lane, b] = here(u, i)
            elif kind == "side":
                for side_of, value in ((0, here), (1, arrived)):
                    @pl.when(hi == side_of)
                    def _():
                        for i, (a, lane, b) in enumerate(blocks):
                            band[a, 3 - 2 * core if lane else 2, b] = value(u, i)
            elif kind == "cross":
                for i, (a, lane, b) in enumerate(blocks):
                    k = 3 - 2 * core if lane else 2
                    band[a, k, b] = band[a, k, b] + arrived(u, i)

        on(u, body)

    z_down = {block: (u, i) for u in range(len(UNITS)) if UNITS[u][0] == "z"
              for i, block in enumerate(UNITS[u][3][:NB])}

    def z_place(u):
        def body():
            for i, (a, lane, b) in enumerate(UNITS[u][3][NB:]):
                band[a, 3 if lane else 4, b] = here(*z_down[(a, lane, b)]) + arrived(u, NB + i)

        on(u, body)

    def put(u, i, block):
        for g in range(2 * NY):
            at = pl.ds(BASE[u] * 128 + (g * COUNT[u] + i) * rows, rows)
            prod[at] = block[g * rows:(g + 1) * rows]

    def put_grid(u, out, rows_of, cols_of):
        for i, (a, lane, b) in enumerate(UNITS[u][3]):
            if a in rows_of and b in cols_of:
                r, c = rows_of.index(a) * 128, cols_of.index(b) * 256 + lane * 128
                put(u, i, out[r:r + 128, c:c + 128])

    def dot(a, b):
        return jnp.dot(a, b, preferred_element_type=jnp.float32)

    out = dot(left[0], alone[0]) + dot(odd_t[...], alone[1])
    for b in range(NB):
        for a in range(NB):
            put(0, b * NB + a, out[a * 128:(a + 1) * 128, b * 128:(b + 1) * 128])
    g_own[...] = out[NB * 128:NB * 128 + 8]
    send(0)

    def g_copy(dy):
        return remote(g_own, g_in.at[y], s_gs.at[dy - 1], s_gr.at[dy - 1], ydev(dy))

    def g_recv(dy):
        return remote(g_own, g_in.at[lax.rem(y - dy + NY, NY)], s_gs.at[dy - 1], s_gr.at[dy - 1], ydev(dy))

    gx_copy = remote(g_sum, g_x, s_gs.at[NY - 1], s_gr.at[NY - 1], xl_pair)
    for dy in range(1, NY):
        g_copy(dy).start()
    g_in[y] = g_own[...]

    for cp in t_copy:
        cp.wait_recv()
    mt_copy.start()
    far_load = pltpu.make_async_copy(far_tab, far_smem, s_tl.at[0])
    far_load.start()
    far_load.wait()
    for cp in m_copy:
        cp.wait_recv()

    @pl.when(core == 0)
    def _():
        for b in range(NB):
            fill_alone(mate0, far_table(0, 0), b, 0)
            fill_alone(mate1, far_table(0, 1), b, 1)
        rows_of = pl.ds(0, NB * 128)
        out = dot(left[0, rows_of], alone[0]) + dot(odd_t[rows_of], alone[1])
        for b in range(NB):
            for a in range(NB):
                put(1, b * NB + a, out[a * 128:(a + 1) * 128, b * 128:(b + 1) * 128])

    send(1)
    for b in range(NB):
        fill(pk1, own_table(1), b, 1, 0)
        fill(mate1, far_table(0, 1), b, 1, 1)
    mt_copy.wait_recv()
    mate_load = pltpu.make_async_copy(mate_tab, mate_smem, s_tl.at[1])
    mate_load.start()
    mate_load.wait()

    def step_units(s):
        return [u for u in range(len(UNITS)) if UNITS[u][2] == s]

    for s in range(NB):
        side, cross, z_self, z_mate = step_units(s)
        d_copy[s].wait_recv()
        od_copy[s].start()
        a_copy0[s].wait_recv()
        oa_copy[s].start()

        fill(pan_d, far_table(1, 0), s, 0, 0)
        fill(pan_a, lambda b, t: far_smem[3, hi * 4 + b, t], s, 2, 0)

        def turn_tile(i, carry):
            turned_a[s][i] = pan_a[s][i].T
            return carry

        lax.fori_loop(0, half, turn_tile, 0, unroll=2)
        turn(turned_a, lambda b, t: far_smem[3, hi * 4 + b, t], s, put_cross(s))
        u_copy[s].wait_recv()
        turn(pan_u, far_table(2, 1), s, put_left(1, s))
        od_copy[s].wait_recv()
        fill(pan_od, mate_table(1, 0), s, 0, 1)
        oa_copy[s].wait_recv()
        fill(pan_oa, lambda b, t: mate_smem[2, hi * 4 + b, t], s, 2, 1)

        upto, now = list(range(s + 1)), pl.ds(s * 256, 256)
        put_grid(cross, dot(cross_t[pl.ds(0, 128 * (s + 1)), :], dense[hi, :, now]), upto, [s])
        if s > 0:
            put_grid(cross, dot(cross_t[pl.ds(128 * s, 128), :], dense[hi, :, pl.ds(0, 256 * s)]),
                     [s], list(range(s)))
        send(cross)
        put_grid(side, dot(left[hi, pl.ds(0, 128 * (s + 1)), :], dense[2, :, now]), upto, [s])
        if s > 0:
            put_grid(side, dot(left[hi, pl.ds(128 * s, 128), :], dense[2, :, pl.ds(0, 256 * s)]),
                     [s], list(range(s)))
        send(side)
        down = dot(left[0, pl.ds(0, NB * 128), :], dense[0, :, now])
        up = dot(left[1, pl.ds(128 * s, 128), :], dense[1])
        for i in range(NB):
            for lane, u in enumerate((z_self, z_mate)):
                put(u, i, down[i * 128:(i + 1) * 128, lane * 128:(lane + 1) * 128])
                put(u, NB + i, up[:, i * 256 + lane * 128:i * 256 + (lane + 1) * 128])
        send(z_self)
        send(z_mate)
        if s == 0:
            for dy in range(1, NY):
                g_recv(dy).wait_recv()
            g_sum[...] = ((g_in[0] + g_in[1]) + g_in[2]) + g_in[3]
            gx_copy.start()
        for u in step_units(s - 1):
            y_finish(u)
        if s > 0:
            for u in step_units(s - 2):
                fin_finish(u)

    gx_copy.wait_recv()
    for b in range(NB):
        at = pl.ds(b * 128, 128)
        grad[pl.ds(b, 1), :] = g_sum[pl.ds(0, 1), at] + g_x[pl.ds(0, 1), at]
    for u in step_units(NB - 2):
        fin_finish(u)
    for u in step_units(NB - 1):
        y_finish(u)
    for u in step_units(NB - 1):
        fin_finish(u)
    for u in range(len(UNITS)):
        if UNITS[u][0] == "z":
            z_place(u)

    for cp in t_copy + [mt_copy] + d_copy + u_copy + a_copy0 + m_copy + od_copy + oa_copy:
        cp.wait_send()
    for u in range(len(UNITS)):
        def drain():
            for dy in range(1, NY):
                y_copy(u, dy).wait_send()
            each(u, lambda cp: cp.wait_send())

        on(u, drain)
    for dy in range(1, NY):
        g_copy(dy).wait_send()
    gx_copy.wait_send()


def on_device(jacobian_tiles, tip_lists, counts, residual):
    _, blocks, slots, tile, _ = jacobian_tiles.shape
    depth = residual.shape[1]
    rows = tile // lax.axis_size("freq")
    n = len(UNITS)
    width = blocks * tile
    dma = pltpu.SemaphoreType.DMA
    bf16, f32, i16, i32 = jnp.bfloat16, jnp.float32, jnp.int16, jnp.int32
    vm = pltpu.VMEM
    half = [vm((slots // 2 + 1, tile, tile), bf16)] * blocks
    coded = TOTAL * tile + n * NY * SCALE_ROWS
    per_block = [dma((blocks,))] * 2
    band, grad = pl.pallas_call(
        band_kernel,
        out_shape=(
            jax.ShapeDtypeStruct((blocks, SHIFTS + 1, blocks, rows, tile), f32),
            jax.ShapeDtypeStruct((blocks, tile), f32),
        ),
        in_specs=[
            pl.BlockSpec(memory_space=pltpu.HBM),
            pl.BlockSpec(memory_space=pltpu.SMEM),
            pl.BlockSpec(memory_space=pltpu.SMEM),
            pl.BlockSpec(memory_space=pltpu.HBM),
        ],
        out_specs=(pl.BlockSpec(memory_space=pltpu.VMEM), pl.BlockSpec(memory_space=pltpu.VMEM)),
        scratch_shapes=[
            [vm((slots, tile, tile), bf16)] * blocks, *[half] * 12,
            vm((1, depth), bf16), vm((2, 8, 128), i32), pltpu.SMEM((2, 8, 128), i32),
            vm((4, 8, 128), i32), pltpu.SMEM((4, 8, 128), i32),
            vm((3, 8, 128), i32), pltpu.SMEM((3, 8, 128), i32),
            vm((3, depth // 2, 2 * width), bf16), vm((2, depth // 2, width), bf16),
            vm((2, width + 16, depth // 2), bf16),
            vm((width + 16, depth // 2), bf16), vm((width, depth // 2), bf16),
            vm((TOTAL * tile, tile), f32), vm((coded, tile), i16), vm((NY - 1, coded // NY, tile), i16),
            vm((TOTAL * 2 * rows, tile), f32), vm((2, TOTAL * rows, tile), f32),
            vm((NY - 1, SCALE_ROWS, tile), f32),
            vm((8, width), f32), vm((NY, 8, width), f32), vm((8, width), f32), vm((8, width), f32),
            dma((blocks + 2,)), dma((5,)), dma((5,)), dma((2,)),
            *per_block, *per_block, *per_block, dma((2 * blocks,)), dma((2 * blocks,)),
            *per_block, *per_block,
            dma((n * (NY - 1),)), dma((n * (NY - 1),)), dma((3 * n,)), dma((3 * n,)),
            dma((NY,)), dma((NY,)),
        ],
        compiler_params=pltpu.CompilerParams(
            collective_id=0, has_side_effects=True, vmem_limit_bytes=63 * 1024 * 1024),
    )(jacobian_tiles.reshape(blocks, slots, tile, tile), tip_lists, counts, residual)
    return band, grad.reshape(width)


def solution(mesh):
    placed = (P("freq", "cells", None, None, None), P("cells", None), P("cells"), P("freq", None))
    return jax.shard_map(
        on_device,
        mesh=mesh,
        in_specs=placed,
        out_specs=(P("cells", None, None, "freq", None), P("cells")),
        check_vma=False,
    )
```

```python
import jax
import jax.numpy as jnp
from jax import lax
from jax.experimental import pallas as pl
from jax.experimental.pallas import tpu as pltpu
from jax.sharding import PartitionSpec as P

SHIFTS = 4
NY = 4
NB = 3
SCALE_ROWS = 16
MESH = pl.DeviceIdType.MESH


def unit_list():
    units = [
        ("own", None, -1, [(a, 0, b) for b in range(NB) for a in range(NB)]),
        ("mate", 0, -1, [(a, 1, b) for b in range(NB) for a in range(NB)]),
    ]
    for s in range(NB):
        grid = [(a, lane, s) for a in range(s + 1) for lane in range(2)]
        grid += [(s, lane, b) for b in range(s) for lane in range(2)]
        units.append(("grid", None, s, grid))
        units.append(("line", None, s, [(i, lane) for i in range(NB) for lane in range(2)]))
        for lane in range(2):
            down = [(a, lane, s) for a in range(NB)]
            up = [(s, lane, b) for b in range(NB)]
            units.append(("z", 1 if lane else None, s, down + up))
    return units


UNITS = unit_list()
COUNT = [len(blocks) for _, _, _, blocks in UNITS]
BASE = [sum(COUNT[:u]) for u in range(len(UNITS))]
TOTAL = sum(COUNT)


def band_kernel(
    jac, tip_lists, counts, resid_hbm, band, grad,
    raw, pk0, pk1, turned0, turned1, mate0, mate1, pan_d, pan_od, pan_u, pan_a, pan_oa, turned_a,
    resid, tab, tab_smem, far_tab, far_smem, mate_tab, mate_smem,
    dense, alone, left, odd_t, prod, coded, y_in, y_sum, fin_in, scale,
    g_own, g_in, g_sum, g_x,
    s_load, s_ts, s_tr, s_tl, s_ds, s_dr, s_us, s_ur, s_as, s_ar, s_ms, s_mr,
    s_ods, s_odr, s_oas, s_oar, s_ys, s_yr, s_fs, s_fr, s_gs, s_gr,
):
    slots = jac.shape[1]
    half = slots // 2
    pairs = resid_hbm.shape[1] // 256
    rows = band.shape[3]
    f = lax.axis_index("freq")
    d = lax.axis_index("cells")
    nf = lax.axis_size("freq")
    nd = lax.axis_size("cells")
    y, xl = f // 2, lax.rem(f, 2)
    hi, core = lax.rem(d // 2, 2), lax.rem(d, 2)

    def ydev(dy):
        return (lax.rem(f + 2 * dy, nf), d)

    below = (f, lax.rem(d - 4 + nd, nd))
    above = (f, lax.rem(d + 4, nd))
    x_pair = (f, d + 2 - 4 * hi)
    core_pair = (f, d + 1 - 2 * core)
    twin = f + 1 - 2 * xl
    xl_pair = (twin, d)

    loads = []
    for b in range(NB):
        loads.append(pltpu.make_async_copy(jac.at[b], raw[b], s_load.at[b]))
    loads.append(pltpu.make_async_copy(resid_hbm, resid, s_load.at[NB]))
    for cp in loads:
        cp.start()

    barrier = pltpu.get_barrier_semaphore()
    partners = [below, above, x_pair, core_pair] + [ydev(dy) for dy in range(1, NY)]
    partners += [xl_pair, (twin, below[1]), (twin, above[1]), (twin, x_pair[1])]
    for dev in partners:
        pl.semaphore_signal(barrier, inc=1, device_id=dev, device_id_type=MESH)

    row = lax.broadcasted_iota(jnp.int32, (8, 128), 0)
    col = lax.broadcasted_iota(jnp.int32, (8, 128), 1)
    place = jnp.full((8, 128), half, jnp.int32)
    slot = jnp.zeros((8, 128), jnp.int32)
    for b in range(NB):
        odd_before = 0
        for p in range(slots):
            name = tip_lists[b, p]
            parity = lax.rem(name, 2)
            rank = jnp.where(parity == 1, odd_before, p - odd_before)
            odd_before = odd_before + parity
            mine = row == parity * 4 + b
            slot = jnp.where(mine & (col == rank), p, slot)
            named = jnp.where(p < counts[b], name // 2, -1)
            place = jnp.where(mine & (col == named), rank, place)
    tab[0] = place
    tab[1] = slot
    own_tab = pltpu.make_async_copy(tab, tab_smem, s_load.at[NB + 1])
    own_tab.start()
    zero = jnp.zeros((128, 128), jnp.bfloat16)
    for panel in (pk0, pk1, turned0, turned1, mate0, mate1,
                  pan_d, pan_od, pan_u, pan_a, pan_oa, turned_a):
        for block in panel:
            block[half] = zero
    for cp in loads:
        cp.wait()
    own_tab.wait()

    def pack(b):
        def step(i, carry):
            even, odd = raw[b][tab_smem[1, b, i]], raw[b][tab_smem[1, 4 + b, i]]
            pk0[b][i], pk1[b][i] = even, odd
            turned0[b][i], turned1[b][i] = even.T, odd.T
            return carry

        lax.fori_loop(0, half, step, 0, unroll=2)

    pack(0)
    pl.semaphore_wait(barrier, len(partners))

    def remote(src, dst, ss, rs, dev):
        return pltpu.make_async_remote_copy(
            src_ref=src, dst_ref=dst, send_sem=ss, recv_sem=rs,
            device_id=dev, device_id_type=MESH)

    live = pl.ds(0, half)

    def panel_copies(src, dst, ss, rs, dev, first=0):
        return [
            remote(src[b].at[live], dst[b].at[live], ss.at[first + b], rs.at[first + b], dev)
            for b in range(NB)]

    d_copy = panel_copies(pk0, pan_d, s_ds, s_dr, below)
    u_copy = panel_copies(turned1, pan_u, s_us, s_ur, above)
    a_copy0 = panel_copies(pk0, pan_a, s_as, s_ar, x_pair)
    a_copy1 = panel_copies(pk1, pan_a, s_as, s_ar, x_pair)
    m_copy = panel_copies(pk0, mate0, s_ms, s_mr, core_pair)
    m_copy += panel_copies(pk1, mate1, s_ms, s_mr, core_pair, NB)
    od_copy = panel_copies(pan_d, pan_od, s_ods, s_odr, core_pair)
    oa_copy = panel_copies(pan_a, pan_oa, s_oas, s_oar, core_pair)
    t_copy = [
        remote(tab.at[0], far_tab.at[i], s_ts.at[i], s_tr.at[i], dev)
        for i, dev in enumerate((core_pair, below, above, x_pair))]
    mt_copy = remote(far_tab.at[pl.ds(1, 3)], mate_tab, s_ts.at[4], s_tr.at[4], core_pair)

    for b in range(NB):
        if b > 0:
            pack(b)
        d_copy[b].start()
        u_copy[b].start()

        @pl.when(hi == 1)
        def _():
            a_copy0[b].start()

        @pl.when(hi == 0)
        def _():
            a_copy1[b].start()

        if b == 0:
            for cp in t_copy:
                cp.start()
        m_copy[b].start()
        m_copy[NB + b].start()

    def turn(panel, table, b, put_tile):
        def step(t, carry):
            at = pl.ds(pl.multiple_of(t * 128, 128), 128)
            put_tile(at, panel[b][table(b, t)])
            return carry

        lax.fori_loop(0, pairs, step, 0, unroll=4)

    def fill(panel, table, b, which, lane):
        at = pl.ds(b * 256 + lane * 128, 128)

        def step(t, carry):
            dense[which, pl.ds(pl.multiple_of(t * 128, 128), 128), at] = panel[b][table(b, t)]
            return carry

        lax.fori_loop(0, pairs, step, 0, unroll=4)

    def fill_alone(panel, table, b, parity):
        at = pl.ds(b * 128, 128)

        def step(t, carry):
            alone[parity, pl.ds(pl.multiple_of(t * 128, 128), 128), at] = panel[b][table(b, t)]
            return carry

        lax.fori_loop(0, pairs, step, 0, unroll=4)

    def own_table(parity):
        return lambda b, t: tab_smem[0, parity * 4 + b, t]

    def far_table(i, parity):
        return lambda b, t: far_smem[i, parity * 4 + b, t]

    def mate_table(i, parity):
        return lambda b, t: mate_smem[i - 1, parity * 4 + b, t]

    def put_left(which, b):
        def put(at, tile):
            left[which, pl.ds(b * 128, 128), at] = tile
        return put

    def put_odd(b):
        def put(at, tile):
            odd_t[pl.ds(b * 128, 128), at] = tile
        return put

    below_rows = pl.ds(NB * 128, 16)
    for t in range(pairs):
        at = pl.ds(t * 128, 128)
        left[0, below_rows, at] = jnp.broadcast_to(resid[:, pl.ds(t * 256, 128)], (16, 128))
        odd_t[below_rows, at] = jnp.broadcast_to(resid[:, pl.ds(t * 256 + 128, 128)], (16, 128))
    for b in range(NB):
        turn(turned0, own_table(0), b, put_left(0, b))
        turn(turned1, own_table(1), b, put_odd(b))
        fill_alone(pk0, own_table(0), b, 0)
        fill_alone(pk1, own_table(1), b, 1)

    def on(u, body):
        which = UNITS[u][1]
        if which is None:
            body()
        else:
            pl.when(core == which)(body)

    def coded_base(u):
        return BASE[u] * 128 + u * NY * SCALE_ROWS

    def y_part(u):
        return COUNT[u] * 2 * rows + SCALE_ROWS

    def y_copy(u, dy):
        part = y_part(u)
        take = pl.ds(pl.multiple_of(coded_base(u) + lax.rem(y + dy, NY) * part, 16), part)
        i = u * (NY - 1) + dy - 1
        return remote(coded.at[take], y_in.at[dy - 1, pl.ds(coded_base(u) // NY, part)],
                      s_ys.at[i], s_yr.at[i], ydev(dy))

    def sums(u, half_of, first, n):
        at = BASE[u] * 2 * rows + half_of * COUNT[u] * rows + first * rows
        return pl.ds(pl.multiple_of(at, 8), n * rows)

    def landed(u, first, n):
        return pl.ds((BASE[u] + first) * rows, n * rows)

    def owner_copies(u):
        kind, n = UNITS[u][0], COUNT[u]

        def copy(i, from_other, first, n, dev):
            src = y_sum.at[sums(u, 1 - xl if from_other else xl, first, n)]
            return remote(src, fin_in.at[i, landed(u, first, n)],
                          s_fs.at[5 * u + i], s_fr.at[5 * u + i], dev)

        if kind == "line":
            return [(0, 0, copy(2, 1, 0, n, xl_pair)),
                    (1, 0, copy(1, 1, 0, n, (twin, x_pair[1]))), (1, 0, copy(0, 0, 0, n, x_pair))]
        if kind == "grid":
            return [(0, 1, copy(1, 1, 0, n, (twin, x_pair[1]))), (0, 1, copy(0, 0, 0, n, x_pair)),
                    (1, 1, copy(4, 1, 0, n, (twin, below[1]))), (1, 1, copy(3, 0, 0, n, below))]
        if kind == "z":
            return [(None, None, copy(2, 1, 0, NB, xl_pair)),
                    (None, None, copy(1, 1, NB, NB, (twin, below[1]))),
                    (None, None, copy(0, 0, NB, NB, below))]
        return [(None, None, copy(2, 1, 0, n, xl_pair))]

    def each(u, receives, act):
        for sends_at, receives_at, cp in owner_copies(u):
            side_of = receives_at if receives else sends_at
            if side_of is None:
                act(cp)
            else:
                pl.when(hi == side_of)(lambda: act(cp))

    line = lax.broadcasted_iota(jnp.int32, (SCALE_ROWS, 128), 0)

    def send(u):
        n = COUNT[u]

        def body():
            parts = [lax.rem(y + dy, NY) for dy in range(1, NY)]

            def code(i, powers):
                new = []
                for part, known in zip(parts, powers):
                    src = pl.multiple_of(BASE[u] * 128 + part * n * 32 + i * 32, 32)
                    dst = pl.multiple_of(coded_base(u) + part * y_part(u) + i * 32, 16)
                    value = prod[pl.ds(src, 32)]
                    top = jnp.maximum(jnp.max(jnp.abs(value), axis=0, keepdims=True), 1e-33)
                    power = jnp.ceil(jnp.log2(top) + 1e-3)
                    up = jnp.exp2(15.0 - power) * (32766.0 / 32768.0)
                    coded[pl.ds(dst, 32)] = jnp.round(value * up).astype(jnp.int32).astype(jnp.int16)
                    new.append(jnp.where(line == i, power, known))
                return tuple(new)

            powers = lax.fori_loop(0, n, code, (jnp.zeros((SCALE_ROWS, 128), jnp.float32),) * (NY - 1))
            for part, power in zip(parts, powers):
                dst = pl.multiple_of(coded_base(u) + part * y_part(u) + n * 32, 16)
                coded[pl.ds(dst, SCALE_ROWS)] = power.astype(jnp.int32).astype(jnp.int16)
            for dy in range(1, NY):
                y_copy(u, dy).start()

        on(u, body)

    def y_finish(u):
        n = COUNT[u]

        def body():
            for dy in range(1, NY):
                y_copy(u, dy).wait_recv()
                power = y_in[dy - 1, pl.ds(coded_base(u) // NY + n * 32, SCALE_ROWS)]
                power = power.astype(jnp.int32).astype(jnp.float32)
                scale[dy - 1] = jnp.exp2(power - 15.0) * (32768.0 / 32766.0)

            def step(i, carry):
                at = pl.ds(pl.multiple_of(BASE[u] * 128 + y * n * 32 + i * 32, 32), 32)
                total = prod[at]
                for dy in range(1, NY):
                    src = pl.ds(pl.multiple_of(coded_base(u) // NY + i * 32, 16), 32)
                    part = y_in[dy - 1, src].astype(jnp.int32).astype(jnp.float32)
                    total = total + part * scale[dy - 1, pl.ds(i, 1)]
                y_sum[pl.ds(pl.multiple_of(BASE[u] * 32 + i * 32, 32), 32)] = total
                return carry

            lax.fori_loop(0, n, step, 0)
            each(u, False, lambda cp: cp.start())

        on(u, body)

    def here(u, i):
        return y_sum[sums(u, xl, i, 1)] + fin_in[2, landed(u, i, 1)]

    def arrived(u, i, first=0):
        return fin_in[first, landed(u, i, 1)] + fin_in[first + 1, landed(u, i, 1)]

    def unit_of(kind, s, which=None):
        return next(u for u in range(len(UNITS))
                    if UNITS[u][0] == kind and UNITS[u][1] == which and UNITS[u][2] == s)

    def fin_finish(s):
        for u in step_units(s):
            on(u, lambda: each(u, True, lambda cp: cp.wait_recv()))
        if s < 0:
            for u in step_units(s):
                def copy_out():
                    for i, (a, lane, b) in enumerate(UNITS[u][3]):
                        band[a, lane, b] = here(u, i)
                on(u, copy_out)
            return
        done = [(a, b) for a in range(NB) for b in range(NB) if max(a, b) == s]

        def k_of(lane):
            return 3 - 2 * core if lane else 2

        @pl.when(hi == 0)
        def _():
            for a, b in done:
                for lane in range(2):
                    band[a, k_of(lane), b] = (here(unit_of("line", b), 2 * a + lane)
                                              + arrived(unit_of("line", a), 2 * b + lane))

        @pl.when(hi == 1)
        def _():
            u = unit_of("grid", s)
            for i, (a, lane, b) in enumerate(UNITS[u][3]):
                band[a, k_of(lane), b] = arrived(u, i) + arrived(u, i, 3)

        for lane, which in enumerate((None, 1)):
            def z_blocks():
                for a, b in done:
                    band[a, 3 if lane else 4, b] = (here(unit_of("z", b, which), a)
                                                    + arrived(unit_of("z", a, which), NB + b))
            on(unit_of("z", s, which), z_blocks)

    def step_units(s):
        return [u for u in range(len(UNITS)) if UNITS[u][2] == s]

    def put(u, i, block):
        for g in range(2 * NY):
            at = pl.ds(BASE[u] * 128 + (g * COUNT[u] + i) * rows, rows)
            prod[at] = block[g * rows:(g + 1) * rows]

    def put_grid(u, out, rows_of, cols_of):
        for i, (a, lane, b) in enumerate(UNITS[u][3]):
            if a in rows_of and b in cols_of:
                r, c = rows_of.index(a) * 128, cols_of.index(b) * 256 + lane * 128
                put(u, i, out[r:r + 128, c:c + 128])

    def dot(a, b):
        return jnp.dot(a, b, preferred_element_type=jnp.float32)

    out = dot(left[0], alone[0]) + dot(odd_t[...], alone[1])
    for b in range(NB):
        for a in range(NB):
            put(0, b * NB + a, out[a * 128:(a + 1) * 128, b * 128:(b + 1) * 128])
    g_own[...] = out[NB * 128:NB * 128 + 8]
    send(0)

    def g_copy(dy):
        return remote(g_own, g_in.at[y], s_gs.at[dy - 1], s_gr.at[dy - 1], ydev(dy))

    def g_recv(dy):
        return remote(g_own, g_in.at[lax.rem(y - dy + NY, NY)], s_gs.at[dy - 1], s_gr.at[dy - 1], ydev(dy))

    gx_copy = remote(g_sum, g_x, s_gs.at[NY - 1], s_gr.at[NY - 1], xl_pair)
    for dy in range(1, NY):
        g_copy(dy).start()
    g_in[y] = g_own[...]

    for cp in t_copy:
        cp.wait_recv()
    mt_copy.start()
    far_load = pltpu.make_async_copy(far_tab, far_smem, s_tl.at[0])
    far_load.start()
    far_load.wait()
    for cp in m_copy:
        cp.wait_recv()

    @pl.when(core == 0)
    def _():
        for b in range(NB):
            fill_alone(mate0, far_table(0, 0), b, 0)
            fill_alone(mate1, far_table(0, 1), b, 1)
        rows_of = pl.ds(0, NB * 128)
        out = dot(left[0, rows_of], alone[0]) + dot(odd_t[rows_of], alone[1])
        for b in range(NB):
            for a in range(NB):
                put(1, b * NB + a, out[a * 128:(a + 1) * 128, b * 128:(b + 1) * 128])

    send(1)
    for b in range(NB):
        fill(pk1, own_table(1), b, 1, 0)
        fill(mate1, far_table(0, 1), b, 1, 1)
    mt_copy.wait_recv()
    mate_load = pltpu.make_async_copy(mate_tab, mate_smem, s_tl.at[1])
    mate_load.start()
    mate_load.wait()

    for s in range(NB):
        grid, line_of, z_self, z_mate = step_units(s)
        d_copy[s].wait_recv()
        od_copy[s].start()
        a_copy0[s].wait_recv()
        oa_copy[s].start()

        fill(pan_d, far_table(1, 0), s, 0, 0)
        fill(pan_a, lambda b, t: far_smem[3, hi * 4 + b, t], s, 2, 0)

        def turn_tile(i, carry):
            turned_a[s][i] = pan_a[s][i].T
            return carry

        lax.fori_loop(0, half, turn_tile, 0, unroll=2)
        turn(turned_a, lambda b, t: far_smem[3, hi * 4 + b, t], s, put_left(2, s))
        u_copy[s].wait_recv()
        turn(pan_u, far_table(2, 1), s, put_left(1, s))
        od_copy[s].wait_recv()
        fill(pan_od, mate_table(1, 0), s, 0, 1)
        oa_copy[s].wait_recv()
        fill(pan_oa, lambda b, t: mate_smem[2, hi * 4 + b, t], s, 2, 1)

        upto, now = list(range(s + 1)), pl.ds(s * 256, 256)
        put_grid(grid, dot(left[2 - hi, pl.ds(0, 128 * (s + 1)), :], dense[2 * hi, :, now]), upto, [s])
        if s > 0:
            put_grid(grid, dot(left[2 - hi, pl.ds(128 * s, 128), :], dense[2 * hi, :, pl.ds(0, 256 * s)]),
                     [s], list(range(s)))
        send(grid)

        @pl.when(hi == 0)
        def _():
            out = dot(left[0, pl.ds(0, NB * 128), :], dense[2, :, now])
            for i, (a, lane) in enumerate(UNITS[line_of][3]):
                put(line_of, i, out[a * 128:(a + 1) * 128, lane * 128:(lane + 1) * 128])

        @pl.when(hi == 1)
        def _():
            out = dot(left[2, pl.ds(128 * s, 128), :], dense[1])
            for i, (b, lane) in enumerate(UNITS[line_of][3]):
                put(line_of, i, out[:, b * 256 + lane * 128:b * 256 + (lane + 1) * 128])

        send(line_of)
        down = dot(left[0, pl.ds(0, NB * 128), :], dense[0, :, now])
        up = dot(left[1, pl.ds(128 * s, 128), :], dense[1])
        for i in range(NB):
            for lane, u in enumerate((z_self, z_mate)):
                put(u, i, down[i * 128:(i + 1) * 128, lane * 128:(lane + 1) * 128])
                put(u, NB + i, up[:, i * 256 + lane * 128:i * 256 + (lane + 1) * 128])
        send(z_self)
        send(z_mate)
        if s == 0:
            for dy in range(1, NY):
                g_recv(dy).wait_recv()
            g_sum[...] = ((g_in[0] + g_in[1]) + g_in[2]) + g_in[3]
            gx_copy.start()
        for u in step_units(s - 1):
            y_finish(u)
        if s > 0:
            fin_finish(s - 2)

    gx_copy.wait_recv()
    for b in range(NB):
        at = pl.ds(b * 128, 128)
        grad[pl.ds(b, 1), :] = g_sum[pl.ds(0, 1), at] + g_x[pl.ds(0, 1), at]
    fin_finish(NB - 2)
    for u in step_units(NB - 1):
        y_finish(u)
    fin_finish(NB - 1)

    for cp in t_copy + [mt_copy] + d_copy + u_copy + a_copy0 + m_copy + od_copy + oa_copy:
        cp.wait_send()
    for u in range(len(UNITS)):
        def drain():
            for dy in range(1, NY):
                y_copy(u, dy).wait_send()
            each(u, False, lambda cp: cp.wait_send())

        on(u, drain)
    for dy in range(1, NY):
        g_copy(dy).wait_send()
    gx_copy.wait_send()


def on_device(jacobian_tiles, tip_lists, counts, residual):
    _, blocks, slots, tile, _ = jacobian_tiles.shape
    depth = residual.shape[1]
    rows = tile // lax.axis_size("freq")
    n = len(UNITS)
    width = blocks * tile
    dma = pltpu.SemaphoreType.DMA
    bf16, f32, i16, i32 = jnp.bfloat16, jnp.float32, jnp.int16, jnp.int32
    vm = pltpu.VMEM
    half = [vm((slots // 2 + 1, tile, tile), bf16)] * blocks
    coded = TOTAL * tile + n * NY * SCALE_ROWS
    per_block = [dma((blocks,))] * 2
    band, grad = pl.pallas_call(
        band_kernel,
        out_shape=(
            jax.ShapeDtypeStruct((blocks, SHIFTS + 1, blocks, rows, tile), f32),
            jax.ShapeDtypeStruct((blocks, tile), f32),
        ),
        in_specs=[
            pl.BlockSpec(memory_space=pltpu.HBM),
            pl.BlockSpec(memory_space=pltpu.SMEM),
            pl.BlockSpec(memory_space=pltpu.SMEM),
            pl.BlockSpec(memory_space=pltpu.HBM),
        ],
        out_specs=(pl.BlockSpec(memory_space=pltpu.VMEM), pl.BlockSpec(memory_space=pltpu.VMEM)),
        scratch_shapes=[
            [vm((slots, tile, tile), bf16)] * blocks, *[half] * 12,
            vm((1, depth), bf16), vm((2, 8, 128), i32), pltpu.SMEM((2, 8, 128), i32),
            vm((4, 8, 128), i32), pltpu.SMEM((4, 8, 128), i32),
            vm((3, 8, 128), i32), pltpu.SMEM((3, 8, 128), i32),
            vm((3, depth // 2, 2 * width), bf16), vm((2, depth // 2, width), bf16),
            vm((3, width + 16, depth // 2), bf16), vm((width + 16, depth // 2), bf16),
            vm((TOTAL * tile, tile), f32), vm((coded, tile), i16), vm((NY - 1, coded // NY, tile), i16),
            vm((TOTAL * 2 * rows, tile), f32), vm((5, TOTAL * rows, tile), f32),
            vm((NY - 1, SCALE_ROWS, tile), f32),
            vm((8, width), f32), vm((NY, 8, width), f32), vm((8, width), f32), vm((8, width), f32),
            dma((blocks + 2,)), dma((5,)), dma((5,)), dma((2,)),
            *per_block, *per_block, *per_block, dma((2 * blocks,)), dma((2 * blocks,)),
            *per_block, *per_block,
            dma((n * (NY - 1),)), dma((n * (NY - 1),)), dma((5 * n,)), dma((5 * n,)),
            dma((NY,)), dma((NY,)),
        ],
        compiler_params=pltpu.CompilerParams(
            collective_id=0, has_side_effects=True, vmem_limit_bytes=63 * 1024 * 1024),
    )(jacobian_tiles.reshape(blocks, slots, tile, tile), tip_lists, counts, residual)
    return band, grad.reshape(width)


def solution(mesh):
    placed = (P("freq", "cells", None, None, None), P("cells", None), P("cells"), P("freq", None))
    return jax.shard_map(
        on_device,
        mesh=mesh,
        in_specs=placed,
        out_specs=(P("cells", None, None, "freq", None), P("cells")),
        check_vma=False,
    )
```

```python
import jax
import jax.numpy as jnp
from jax import lax
from jax.experimental import pallas as pl
from jax.experimental.pallas import tpu as pltpu
from jax.sharding import PartitionSpec as P

SHIFTS = 4
NY = 4
NB = 3
SCALE_ROWS = 16
MESH = pl.DeviceIdType.MESH


def unit_list():
    units = [
        ("own", None, -1, [(a, 0, b) for b in range(NB) for a in range(NB)]),
        ("mate", 0, -1, [(a, 1, b) for b in range(NB) for a in range(NB)]),
    ]
    for s in range(NB):
        grid = [(a, lane, s) for a in range(s + 1) for lane in range(2)]
        grid += [(s, lane, b) for b in range(s) for lane in range(2)]
        units.append(("grid", None, s, grid))
        units.append(("line", None, s, [(i, lane) for i in range(NB) for lane in range(2)]))
        for lane in range(2):
            down = [(a, lane, s) for a in range(NB)]
            up = [(s, lane, b) for b in range(NB)]
            units.append(("z", 1 if lane else None, s, down + up))
    return units


UNITS = unit_list()
COUNT = [len(blocks) for _, _, _, blocks in UNITS]
BASE = [sum(COUNT[:u]) for u in range(len(UNITS))]
TOTAL = sum(COUNT)


def band_kernel(
    jac, tip_lists, counts, resid_hbm, band, grad,
    raw, pk0, pk1, turned0, turned1, mate0, mate1, pan_d, pan_od, pan_u, pan_a, pan_oa, turned_a,
    resid, tab, tab_smem, far_tab, far_smem, mate_tab, mate_smem,
    dense, alone, left, odd_t, prod, coded, y_in, y_sum, fin_in, scale,
    g_own, g_in, g_sum, g_x,
    s_load, s_ts, s_tr, s_tl, s_ds, s_dr, s_us, s_ur, s_as, s_ar, s_ms, s_mr,
    s_ods, s_odr, s_oas, s_oar, s_ys, s_yr, s_fs, s_fr, s_gs, s_gr,
):
    slots = jac.shape[1]
    half = slots // 2
    pairs = resid_hbm.shape[1] // 256
    rows = band.shape[3]
    f = lax.axis_index("freq")
    d = lax.axis_index("cells")
    nf = lax.axis_size("freq")
    nd = lax.axis_size("cells")
    y, xl = f // 2, lax.rem(f, 2)
    hi, core = lax.rem(d // 2, 2), lax.rem(d, 2)

    def ydev(dy):
        return (lax.rem(f + 2 * dy, nf), d)

    below = (f, lax.rem(d - 4 + nd, nd))
    above = (f, lax.rem(d + 4, nd))
    x_pair = (f, d + 2 - 4 * hi)
    core_pair = (f, d + 1 - 2 * core)
    twin = f + 1 - 2 * xl
    xl_pair = (twin, d)

    loads = []
    for b in range(NB):
        loads.append(pltpu.make_async_copy(jac.at[b], raw[b], s_load.at[b]))
    loads.append(pltpu.make_async_copy(resid_hbm, resid, s_load.at[NB]))
    for cp in loads:
        cp.start()

    barrier = pltpu.get_barrier_semaphore()
    partners = [below, above, x_pair, core_pair] + [ydev(dy) for dy in range(1, NY)]
    partners += [xl_pair, (twin, below[1]), (twin, above[1]), (twin, x_pair[1])]
    for dev in partners:
        pl.semaphore_signal(barrier, inc=1, device_id=dev, device_id_type=MESH)

    row = lax.broadcasted_iota(jnp.int32, (8, 128), 0)
    col = lax.broadcasted_iota(jnp.int32, (8, 128), 1)
    place = jnp.full((8, 128), half, jnp.int32)
    slot = jnp.zeros((8, 128), jnp.int32)
    for b in range(NB):
        odd_before = 0
        for p in range(slots):
            name = tip_lists[b, p]
            parity = lax.rem(name, 2)
            rank = jnp.where(parity == 1, odd_before, p - odd_before)
            odd_before = odd_before + parity
            mine = row == parity * 4 + b
            slot = jnp.where(mine & (col == rank), p, slot)
            named = jnp.where(p < counts[b], name // 2, -1)
            place = jnp.where(mine & (col == named), rank, place)
    tab[0] = place
    tab[1] = slot
    own_tab = pltpu.make_async_copy(tab, tab_smem, s_load.at[NB + 1])
    own_tab.start()
    zero = jnp.zeros((128, 128), jnp.bfloat16)
    for panel in (pk0, pk1, turned0, turned1, mate0, mate1,
                  pan_d, pan_od, pan_u, pan_a, pan_oa, turned_a):
        for block in panel:
            block[half] = zero
    for cp in loads:
        cp.wait()
    own_tab.wait()

    def pack(b):
        def step(i, carry):
            even, odd = raw[b][tab_smem[1, b, i]], raw[b][tab_smem[1, 4 + b, i]]
            pk0[b][i], pk1[b][i] = even, odd
            return carry

        lax.fori_loop(0, half, step, 0, unroll=2)

    def pack_turned(b):
        def step(i, carry):
            turned0[b][i], turned1[b][i] = pk0[b][i].T, pk1[b][i].T
            return carry

        lax.fori_loop(0, half, step, 0, unroll=2)

    pack(0)
    pl.semaphore_wait(barrier, len(partners))

    def remote(src, dst, ss, rs, dev):
        return pltpu.make_async_remote_copy(
            src_ref=src, dst_ref=dst, send_sem=ss, recv_sem=rs,
            device_id=dev, device_id_type=MESH)

    live = pl.ds(0, half)

    def panel_copies(src, dst, ss, rs, dev, first=0):
        return [
            remote(src[b].at[live], dst[b].at[live], ss.at[first + b], rs.at[first + b], dev)
            for b in range(NB)]

    d_copy = panel_copies(pk0, pan_d, s_ds, s_dr, below)
    u_copy = panel_copies(turned1, pan_u, s_us, s_ur, above)
    a_copy0 = panel_copies(pk0, pan_a, s_as, s_ar, x_pair)
    a_copy1 = panel_copies(pk1, pan_a, s_as, s_ar, x_pair)
    m_copy = panel_copies(pk0, mate0, s_ms, s_mr, core_pair)
    m_copy += panel_copies(pk1, mate1, s_ms, s_mr, core_pair, NB)
    od_copy = panel_copies(pan_d, pan_od, s_ods, s_odr, core_pair)
    oa_copy = panel_copies(pan_a, pan_oa, s_oas, s_oar, core_pair)
    t_copy = [
        remote(tab.at[0], far_tab.at[i], s_ts.at[i], s_tr.at[i], dev)
        for i, dev in enumerate((core_pair, below, above, x_pair))]
    mt_copy = remote(far_tab.at[pl.ds(1, 3)], mate_tab, s_ts.at[4], s_tr.at[4], core_pair)

    for b in range(NB):
        if b > 0:
            pack(b)
        d_copy[b].start()

        @pl.when(hi == 1)
        def _():
            a_copy0[b].start()

        @pl.when(hi == 0)
        def _():
            a_copy1[b].start()

        pack_turned(b)
        u_copy[b].start()
        if b == 0:
            for cp in t_copy:
                cp.start()
        m_copy[b].start()
        m_copy[NB + b].start()

    def turn(panel, table, b, put_tile):
        def step(t, carry):
            at = pl.ds(pl.multiple_of(t * 128, 128), 128)
            put_tile(at, panel[b][table(b, t)])
            return carry

        lax.fori_loop(0, pairs, step, 0, unroll=4)

    def fill(panel, table, b, which, lane):
        at = pl.ds(b * 256 + lane * 128, 128)

        def step(t, carry):
            dense[which, pl.ds(pl.multiple_of(t * 128, 128), 128), at] = panel[b][table(b, t)]
            return carry

        lax.fori_loop(0, pairs, step, 0, unroll=4)

    def fill_alone(panel, table, b, parity):
        at = pl.ds(b * 128, 128)

        def step(t, carry):
            alone[parity, pl.ds(pl.multiple_of(t * 128, 128), 128), at] = panel[b][table(b, t)]
            return carry

        lax.fori_loop(0, pairs, step, 0, unroll=4)

    def own_table(parity):
        return lambda b, t: tab_smem[0, parity * 4 + b, t]

    def far_table(i, parity):
        return lambda b, t: far_smem[i, parity * 4 + b, t]

    def mate_table(i, parity):
        return lambda b, t: mate_smem[i - 1, parity * 4 + b, t]

    def put_left(which, b):
        def put(at, tile):
            left[which, pl.ds(b * 128, 128), at] = tile
        return put

    def put_odd(b):
        def put(at, tile):
            odd_t[pl.ds(b * 128, 128), at] = tile
        return put

    below_rows = pl.ds(NB * 128, 16)
    for t in range(pairs):
        at = pl.ds(t * 128, 128)
        left[0, below_rows, at] = jnp.broadcast_to(resid[:, pl.ds(t * 256, 128)], (16, 128))
        odd_t[below_rows, at] = jnp.broadcast_to(resid[:, pl.ds(t * 256 + 128, 128)], (16, 128))
    for b in range(NB):
        turn(turned0, own_table(0), b, put_left(0, b))
        turn(turned1, own_table(1), b, put_odd(b))
        fill_alone(pk0, own_table(0), b, 0)
        fill_alone(pk1, own_table(1), b, 1)

    def on(u, body):
        which = UNITS[u][1]
        if which is None:
            body()
        else:
            pl.when(core == which)(body)

    def coded_base(u):
        return BASE[u] * 128 + u * NY * SCALE_ROWS

    def y_part(u):
        return COUNT[u] * 2 * rows + SCALE_ROWS

    def y_copy(u, dy):
        part = y_part(u)
        take = pl.ds(pl.multiple_of(coded_base(u) + lax.rem(y + dy, NY) * part, 16), part)
        i = u * (NY - 1) + dy - 1
        return remote(coded.at[take], y_in.at[dy - 1, pl.ds(coded_base(u) // NY, part)],
                      s_ys.at[i], s_yr.at[i], ydev(dy))

    def sums(u, half_of, first, n):
        at = BASE[u] * 2 * rows + half_of * COUNT[u] * rows + first * rows
        return pl.ds(pl.multiple_of(at, 8), n * rows)

    def landed(u, first, n):
        return pl.ds((BASE[u] + first) * rows, n * rows)

    def owner_copies(u):
        kind, n = UNITS[u][0], COUNT[u]

        def copy(i, from_other, first, n, dev):
            src = y_sum.at[sums(u, 1 - xl if from_other else xl, first, n)]
            return remote(src, fin_in.at[i, landed(u, first, n)],
                          s_fs.at[5 * u + i], s_fr.at[5 * u + i], dev)

        if kind == "line":
            return [(0, 0, copy(2, 1, 0, n, xl_pair)),
                    (1, 0, copy(1, 1, 0, n, (twin, x_pair[1]))), (1, 0, copy(0, 0, 0, n, x_pair))]
        if kind == "grid":
            return [(0, 1, copy(1, 1, 0, n, (twin, x_pair[1]))), (0, 1, copy(0, 0, 0, n, x_pair)),
                    (1, 1, copy(4, 1, 0, n, (twin, below[1]))), (1, 1, copy(3, 0, 0, n, below))]
        if kind == "z":
            return [(None, None, copy(2, 1, 0, NB, xl_pair)),
                    (None, None, copy(1, 1, NB, NB, (twin, below[1]))),
                    (None, None, copy(0, 0, NB, NB, below))]
        return [(None, None, copy(2, 1, 0, n, xl_pair))]

    def each(u, receives, act):
        for sends_at, receives_at, cp in owner_copies(u):
            side_of = receives_at if receives else sends_at
            if side_of is None:
                act(cp)
            else:
                pl.when(hi == side_of)(lambda: act(cp))

    line = lax.broadcasted_iota(jnp.int32, (SCALE_ROWS, 128), 0)

    def send(u):
        n = COUNT[u]

        def body():
            parts = [lax.rem(y + dy, NY) for dy in range(1, NY)]

            def code(i, powers):
                new = []
                for part, known in zip(parts, powers):
                    src = pl.multiple_of(BASE[u] * 128 + part * n * 32 + i * 32, 32)
                    dst = pl.multiple_of(coded_base(u) + part * y_part(u) + i * 32, 16)
                    value = prod[pl.ds(src, 32)]
                    top = jnp.maximum(jnp.max(jnp.abs(value), axis=0, keepdims=True), 1e-33)
                    power = jnp.ceil(jnp.log2(top) + 1e-3)
                    up = jnp.exp2(15.0 - power) * (32766.0 / 32768.0)
                    coded[pl.ds(dst, 32)] = jnp.round(value * up).astype(jnp.int32).astype(jnp.int16)
                    new.append(jnp.where(line == i, power, known))
                return tuple(new)

            powers = lax.fori_loop(0, n, code, (jnp.zeros((SCALE_ROWS, 128), jnp.float32),) * (NY - 1),
                                   unroll=2 if n % 2 == 0 else 3)
            for part, power in zip(parts, powers):
                dst = pl.multiple_of(coded_base(u) + part * y_part(u) + n * 32, 16)
                coded[pl.ds(dst, SCALE_ROWS)] = power.astype(jnp.int32).astype(jnp.int16)
            for dy in range(1, NY):
                y_copy(u, dy).start()

        on(u, body)

    def y_finish(u):
        n = COUNT[u]

        def body():
            for dy in range(1, NY):
                y_copy(u, dy).wait_recv()
                power = y_in[dy - 1, pl.ds(coded_base(u) // NY + n * 32, SCALE_ROWS)]
                power = power.astype(jnp.int32).astype(jnp.float32)
                scale[dy - 1] = jnp.exp2(power - 15.0) * (32768.0 / 32766.0)

            def step(i, carry):
                at = pl.ds(pl.multiple_of(BASE[u] * 128 + y * n * 32 + i * 32, 32), 32)
                total = prod[at]
                for dy in range(1, NY):
                    src = pl.ds(pl.multiple_of(coded_base(u) // NY + i * 32, 16), 32)
                    part = y_in[dy - 1, src].astype(jnp.int32).astype(jnp.float32)
                    total = total + part * scale[dy - 1, pl.ds(i, 1)]
                y_sum[pl.ds(pl.multiple_of(BASE[u] * 32 + i * 32, 32), 32)] = total
                return carry

            lax.fori_loop(0, n, step, 0, unroll=2 if n % 2 == 0 else 3)
            each(u, False, lambda cp: cp.start())

        on(u, body)

    def here(u, i):
        return y_sum[sums(u, xl, i, 1)] + fin_in[2, landed(u, i, 1)]

    def arrived(u, i, first=0):
        return fin_in[first, landed(u, i, 1)] + fin_in[first + 1, landed(u, i, 1)]

    def unit_of(kind, s, which=None):
        return next(u for u in range(len(UNITS))
                    if UNITS[u][0] == kind and UNITS[u][1] == which and UNITS[u][2] == s)

    def fin_finish(s):
        for u in step_units(s):
            on(u, lambda: each(u, True, lambda cp: cp.wait_recv()))
        if s < 0:
            for u in step_units(s):
                def copy_out():
                    for i, (a, lane, b) in enumerate(UNITS[u][3]):
                        band[a, lane, b] = here(u, i)
                on(u, copy_out)
            return
        done = [(a, b) for a in range(NB) for b in range(NB) if max(a, b) == s]

        def k_of(lane):
            return 3 - 2 * core if lane else 2

        @pl.when(hi == 0)
        def _():
            for a, b in done:
                for lane in range(2):
                    band[a, k_of(lane), b] = (here(unit_of("line", b), 2 * a + lane)
                                              + arrived(unit_of("line", a), 2 * b + lane))

        @pl.when(hi == 1)
        def _():
            u = unit_of("grid", s)
            for i, (a, lane, b) in enumerate(UNITS[u][3]):
                band[a, k_of(lane), b] = arrived(u, i) + arrived(u, i, 3)

        for lane, which in enumerate((None, 1)):
            def z_blocks():
                for a, b in done:
                    band[a, 3 if lane else 4, b] = (here(unit_of("z", b, which), a)
                                                    + arrived(unit_of("z", a, which), NB + b))
            on(unit_of("z", s, which), z_blocks)

    def step_units(s):
        return [u for u in range(len(UNITS)) if UNITS[u][2] == s]

    def put(u, i, block):
        for g in range(2 * NY):
            at = pl.ds(BASE[u] * 128 + (g * COUNT[u] + i) * rows, rows)
            prod[at] = block[g * rows:(g + 1) * rows]

    def put_grid(u, out, rows_of, cols_of):
        for i, (a, lane, b) in enumerate(UNITS[u][3]):
            if a in rows_of and b in cols_of:
                r, c = rows_of.index(a) * 128, cols_of.index(b) * 256 + lane * 128
                put(u, i, out[r:r + 128, c:c + 128])

    def dot(a, b):
        return jnp.dot(a, b, preferred_element_type=jnp.float32)

    out = dot(left[0], alone[0]) + dot(odd_t[...], alone[1])
    for b in range(NB):
        for a in range(NB):
            put(0, b * NB + a, out[a * 128:(a + 1) * 128, b * 128:(b + 1) * 128])
    g_own[...] = out[NB * 128:NB * 128 + 8]
    send(0)

    def g_copy(dy):
        return remote(g_own, g_in.at[y], s_gs.at[dy - 1], s_gr.at[dy - 1], ydev(dy))

    def g_recv(dy):
        return remote(g_own, g_in.at[lax.rem(y - dy + NY, NY)], s_gs.at[dy - 1], s_gr.at[dy - 1], ydev(dy))

    gx_copy = remote(g_sum, g_x, s_gs.at[NY - 1], s_gr.at[NY - 1], xl_pair)
    for dy in range(1, NY):
        g_copy(dy).start()
    g_in[y] = g_own[...]

    for cp in t_copy:
        cp.wait_recv()
    mt_copy.start()
    far_load = pltpu.make_async_copy(far_tab, far_smem, s_tl.at[0])
    far_load.start()
    far_load.wait()
    for cp in m_copy:
        cp.wait_recv()

    @pl.when(core == 0)
    def _():
        for b in range(NB):
            fill_alone(mate0, far_table(0, 0), b, 0)
            fill_alone(mate1, far_table(0, 1), b, 1)
        rows_of = pl.ds(0, NB * 128)
        out = dot(left[0, rows_of], alone[0]) + dot(odd_t[rows_of], alone[1])
        for b in range(NB):
            for a in range(NB):
                put(1, b * NB + a, out[a * 128:(a + 1) * 128, b * 128:(b + 1) * 128])

    send(1)
    for b in range(NB):
        fill(pk1, own_table(1), b, 1, 0)
        fill(mate1, far_table(0, 1), b, 1, 1)
    mt_copy.wait_recv()
    mate_load = pltpu.make_async_copy(mate_tab, mate_smem, s_tl.at[1])
    mate_load.start()
    mate_load.wait()

    for s in range(NB):
        grid, line_of, z_self, z_mate = step_units(s)
        d_copy[s].wait_recv()
        od_copy[s].start()
        a_copy0[s].wait_recv()
        oa_copy[s].start()

        fill(pan_d, far_table(1, 0), s, 0, 0)
        fill(pan_a, lambda b, t: far_smem[3, hi * 4 + b, t], s, 2, 0)

        def turn_tile(i, carry):
            turned_a[s][i] = pan_a[s][i].T
            return carry

        lax.fori_loop(0, half, turn_tile, 0, unroll=2)
        turn(turned_a, lambda b, t: far_smem[3, hi * 4 + b, t], s, put_left(2, s))
        u_copy[s].wait_recv()
        turn(pan_u, far_table(2, 1), s, put_left(1, s))
        od_copy[s].wait_recv()
        fill(pan_od, mate_table(1, 0), s, 0, 1)
        oa_copy[s].wait_recv()
        fill(pan_oa, lambda b, t: mate_smem[2, hi * 4 + b, t], s, 2, 1)

        upto, now = list(range(s + 1)), pl.ds(s * 256, 256)
        put_grid(grid, dot(left[2 - hi, pl.ds(0, 128 * (s + 1)), :], dense[2 * hi, :, now]), upto, [s])
        if s > 0:
            put_grid(grid, dot(left[2 - hi, pl.ds(128 * s, 128), :], dense[2 * hi, :, pl.ds(0, 256 * s)]),
                     [s], list(range(s)))
        send(grid)

        @pl.when(hi == 0)
        def _():
            out = dot(left[0, pl.ds(0, NB * 128), :], dense[2, :, now])
            for i, (a, lane) in enumerate(UNITS[line_of][3]):
                put(line_of, i, out[a * 128:(a + 1) * 128, lane * 128:(lane + 1) * 128])

        @pl.when(hi == 1)
        def _():
            out = dot(left[2, pl.ds(128 * s, 128), :], dense[1])
            for i, (b, lane) in enumerate(UNITS[line_of][3]):
                put(line_of, i, out[:, b * 256 + lane * 128:b * 256 + (lane + 1) * 128])

        send(line_of)
        down = dot(left[0, pl.ds(0, NB * 128), :], dense[0, :, now])
        up = dot(left[1, pl.ds(128 * s, 128), :], dense[1])
        for i in range(NB):
            for lane, u in enumerate((z_self, z_mate)):
                put(u, i, down[i * 128:(i + 1) * 128, lane * 128:(lane + 1) * 128])
                put(u, NB + i, up[:, i * 256 + lane * 128:i * 256 + (lane + 1) * 128])
        send(z_self)
        send(z_mate)
        if s == 0:
            for dy in range(1, NY):
                g_recv(dy).wait_recv()
            g_sum[...] = ((g_in[0] + g_in[1]) + g_in[2]) + g_in[3]
            gx_copy.start()
        for u in step_units(s - 1):
            y_finish(u)
        if s > 0:
            fin_finish(s - 2)

    gx_copy.wait_recv()
    for b in range(NB):
        at = pl.ds(b * 128, 128)
        grad[pl.ds(b, 1), :] = g_sum[pl.ds(0, 1), at] + g_x[pl.ds(0, 1), at]
    fin_finish(NB - 2)
    for u in step_units(NB - 1):
        y_finish(u)
    fin_finish(NB - 1)

    for cp in t_copy + [mt_copy] + d_copy + u_copy + a_copy0 + m_copy + od_copy + oa_copy:
        cp.wait_send()
    for u in range(len(UNITS)):
        def drain():
            for dy in range(1, NY):
                y_copy(u, dy).wait_send()
            each(u, False, lambda cp: cp.wait_send())

        on(u, drain)
    for dy in range(1, NY):
        g_copy(dy).wait_send()
    gx_copy.wait_send()


def on_device(jacobian_tiles, tip_lists, counts, residual):
    _, blocks, slots, tile, _ = jacobian_tiles.shape
    depth = residual.shape[1]
    rows = tile // lax.axis_size("freq")
    n = len(UNITS)
    width = blocks * tile
    dma = pltpu.SemaphoreType.DMA
    bf16, f32, i16, i32 = jnp.bfloat16, jnp.float32, jnp.int16, jnp.int32
    vm = pltpu.VMEM
    half = [vm((slots // 2 + 1, tile, tile), bf16)] * blocks
    coded = TOTAL * tile + n * NY * SCALE_ROWS
    per_block = [dma((blocks,))] * 2
    band, grad = pl.pallas_call(
        band_kernel,
        out_shape=(
            jax.ShapeDtypeStruct((blocks, SHIFTS + 1, blocks, rows, tile), f32),
            jax.ShapeDtypeStruct((blocks, tile), f32),
        ),
        in_specs=[
            pl.BlockSpec(memory_space=pltpu.HBM),
            pl.BlockSpec(memory_space=pltpu.SMEM),
            pl.BlockSpec(memory_space=pltpu.SMEM),
            pl.BlockSpec(memory_space=pltpu.HBM),
        ],
        out_specs=(pl.BlockSpec(memory_space=pltpu.VMEM), pl.BlockSpec(memory_space=pltpu.VMEM)),
        scratch_shapes=[
            [vm((slots, tile, tile), bf16)] * blocks, *[half] * 12,
            vm((1, depth), bf16), vm((2, 8, 128), i32), pltpu.SMEM((2, 8, 128), i32),
            vm((4, 8, 128), i32), pltpu.SMEM((4, 8, 128), i32),
            vm((3, 8, 128), i32), pltpu.SMEM((3, 8, 128), i32),
            vm((3, depth // 2, 2 * width), bf16), vm((2, depth // 2, width), bf16),
            vm((3, width + 16, depth // 2), bf16), vm((width + 16, depth // 2), bf16),
            vm((TOTAL * tile, tile), f32), vm((coded, tile), i16), vm((NY - 1, coded // NY, tile), i16),
            vm((TOTAL * 2 * rows, tile), f32), vm((5, TOTAL * rows, tile), f32),
            vm((NY - 1, SCALE_ROWS, tile), f32),
            vm((8, width), f32), vm((NY, 8, width), f32), vm((8, width), f32), vm((8, width), f32),
            dma((blocks + 2,)), dma((5,)), dma((5,)), dma((2,)),
            *per_block, *per_block, *per_block, dma((2 * blocks,)), dma((2 * blocks,)),
            *per_block, *per_block,
            dma((n * (NY - 1),)), dma((n * (NY - 1),)), dma((5 * n,)), dma((5 * n,)),
            dma((NY,)), dma((NY,)),
        ],
        compiler_params=pltpu.CompilerParams(
            collective_id=0, has_side_effects=True, vmem_limit_bytes=63 * 1024 * 1024),
    )(jacobian_tiles.reshape(blocks, slots, tile, tile), tip_lists, counts, residual)
    return band, grad.reshape(width)


def solution(mesh):
    placed = (P("freq", "cells", None, None, None), P("cells", None), P("cells"), P("freq", None))
    return jax.shard_map(
        on_device,
        mesh=mesh,
        in_specs=placed,
        out_specs=(P("cells", None, None, "freq", None), P("cells")),
        check_vma=False,
    )
```
